128 devices in a mesh: mesh: 32 (over z, y_hi, x), freq: 4 (over y_lo, core).
Axes of the slice: x: 4, y: 4 (y_hi: 2, y_lo: 2; y = y_hi * 2 + y_lo), z: 4, core: 2. Of those that a mesh axis runs over, the one named last changes fastest.
Arguments:
- spectra: float32 [36, 36, 16384], P('freq', None, 'mesh'), may hold values from 0.1 to 2
- coords: float32 [2, 16384], P(None, 'mesh'), may hold values from -5 to 5
- inv_area: float32 [16384], P('mesh'), may hold values from 0.3 to 1
- wind_vector: float32 [2, 16384], P(None, 'mesh'), may hold values from -6 to 6
- neighbours: int32 [8, 16384], P(None, 'mesh'), may hold values from 0 to 767, as said below
- send_nodes: int32 [1024, 8], P('mesh'), may hold values from 0 to 511
- send_count: int32 [1024], P('mesh'), may hold values from 1 to 8, as said below
Outputs:
- updated: float32 [36, 36, 16384], P('freq', None, 'mesh')
The draws below stay inside these ranges and needn't reach their ends.
Inputs may be any that keep to these rules, and one draw needn't show every extreme that they name: `neighbours`: an entry below 512 is a node of the same partition; an entry 512 + q * 8 + c names slot c of the list that partition q sends to this partition, with c below that list's count; slots past a node's degree name the node itself; some node uses all 8 slots. `send_count`: in every draw some partition receives exactly 8 nodes from every partition.
All inputs are finite; a program needn't handle non-finite values.
Results may differ from the reference program's by a relative error of at most 0.00002.
Values sent between devices are 32-bit elements; how exact they have to be, the bound alone decides.
No kernel may reach another device: no remote copies, remote signals or barrier semaphores. Data moves between devices by JAX's collectives and lax.ppermute only.
A program may use at most 64 MiB of HBM per device.

```python
import math
import jax
import jax.numpy as jnp
from jax import lax

NF = 36
ND = 36
K = 8
REACH = 3
SWEEPS = 2
NP = 512
UP_SHIFT = 1
DOWN_SHIFT = 3
CAP = 8
NODES = 16384
PAIRS = 1024


def counts_table(key):
    parts_count = NODES // NP
    key_fill = jax.random.fold_in(key, 11)
    key_full = jax.random.fold_in(key, 12)
    table = jax.random.randint(key_fill, (parts_count, parts_count), 1, CAP + 1)
    crowded = jax.random.randint(key_full, (), 0, parts_count)
    table = jnp.where(jnp.arange(parts_count)[None, :] == crowded, CAP, table)
    return table.reshape(-1).astype(jnp.int32)


def draw_send_count(key, part):
    return counts_table(key)


def draw_neighbours(key, part):
    parts_count = NODES // NP
    counts = counts_table(key)
    node_ids = jnp.arange(NODES, dtype=jnp.int32)
    owner = node_ids // NP
    own_local = node_ids % NP
    degree = jax.random.randint(jax.random.fold_in(key, 21), (NODES,), 3, K + 1)
    degree = jnp.where(node_ids == 0, K, degree)
    slot_ids = jnp.arange(K, dtype=jnp.int32)[:, None]
    kinds = jax.random.randint(jax.random.fold_in(key, 22), (K, NODES), 0, 4)
    local_pick = jax.random.randint(jax.random.fold_in(key, 23), (K, NODES), 0, NP)
    source = jax.random.randint(jax.random.fold_in(key, 24), (K, NODES), 0, parts_count)
    limit = counts[source * parts_count + owner[None, :]]
    place = jax.random.randint(jax.random.fold_in(key, 25), (K, NODES), 0, limit)
    ghost_entry = NP + source * CAP + place
    entry = jnp.where(kinds == 0, ghost_entry, local_pick)
    entry = jnp.where(slot_ids < degree[None, :], entry, own_local[None, :])
    return entry.astype(jnp.int32)


def set_ends(drawn, rng, low, top_value):
    index_at = [jax.random.randint(jax.random.fold_in(rng, axis), (), 0, length) for axis, length in enumerate(drawn.shape)]
    longest = drawn.shape.index(max(drawn.shape))
    beside = index_at[:longest] + [(index_at[longest] + 1) % drawn.shape[longest]] + index_at[longest + 1:]
    return drawn.at[tuple(index_at)].set(low).at[tuple(beside)].set(top_value)


def steps_of(stream_key, extent, split, smallest, high):
    loudness, own = 1.0, jax.random.fold_in(stream_key, 6)
    for position, blocks in split:
        heights = jnp.exp(jax.random.uniform(jax.random.fold_in(own, position), (blocks,), jnp.float32, smallest / len(split), high / len(split)))
        loudness = loudness * jnp.repeat(heights, extent[position] // blocks).reshape([-1 if axis == position else 1 for axis in range(len(extent))])
    return loudness


def centred(key, dims, width, most, pieces=(), held_as=jnp.bfloat16):
    array = jax.random.normal(key, dims, jnp.float32) * width
    if len(pieces) > 0:
        array = steps_of(key, dims, pieces, -0.22, 0.18) * array
    return jnp.clip(array, min=-most, max=most).astype(held_as)


def setup_inputs(seed: int = 0) -> dict:
    keys = jax.random.split(jax.random.key(seed), 8)
    spectra = jnp.clip(jnp.exp(math.log(2.0) - 2.9957323 * jax.random.uniform(keys[0], (NF, ND, NODES), jnp.float32) ** steps_of(keys[0], (NF, ND, NODES), ((0, 4), (2, 32)), -0.2, 0.2)), 0.1, 2.0)
    coords = centred(keys[1], (2, NODES), 1.0, 5.0, ((1, 32),), jnp.float32)
    inv_area = jnp.clip(jnp.exp(math.log(1.0) - 1.2039728 * jax.random.uniform(keys[2], (NODES,), jnp.float32) ** steps_of(keys[2], (NODES,), ((0, 32),), -0.2, 0.2)), 0.3, 1.0)
    wind_vector = centred(keys[3], (2, NODES), 1.5, 6.0, ((1, 32),), jnp.float32)
    neighbours = draw_neighbours(jax.random.fold_in(keys[7], 71), 0)
    send_nodes = set_ends(jax.random.randint(keys[5], (PAIRS, CAP), 0, NP), jax.random.fold_in(keys[5], 1), 0, NP - 1).astype(jnp.int32)
    send_count = draw_send_count(jax.random.fold_in(keys[7], 71), 0)
    return {"spectra": spectra, "coords": coords, "inv_area": inv_area, "wind_vector": wind_vector, "neighbours": neighbours, "send_nodes": send_nodes, "send_count": send_count}


time_step = 0.5
group_scale = 0.8
quad_coupling = 0.25
wind_growth = 0.1
freq_ratio = 1.1


def direction_tables():
    angles = (jnp.arange(ND, dtype=jnp.float32) + 0.5) * (2.0 * math.pi / ND)
    return jnp.cos(angles), jnp.sin(angles)


def source_terms(density, widened, ratios, wind_vector):
    band_count = density.shape[0]
    upper = lax.slice_in_dim(widened, REACH + REACH - 1, REACH + REACH - 1 + band_count, axis=0)
    lower = lax.slice_in_dim(widened, 0, band_count, axis=0)
    upper_left = jnp.roll(upper, -UP_SHIFT, axis=1)
    lower_left = jnp.roll(lower, DOWN_SHIFT, axis=1)
    upper_right = jnp.roll(upper, UP_SHIFT, axis=1)
    lower_right = jnp.roll(lower, -DOWN_SHIFT, axis=1)
    quad = quad_coupling * (density * density * (upper_left + lower_left + upper_right + lower_right)
                            - 2.0 * density * (upper_left * lower_left + upper_right * lower_right))
    cosine, sine = direction_tables()
    along = cosine[:, None] * wind_vector[0][None, :] + sine[:, None] * wind_vector[1][None, :]
    growth = wind_growth * jnp.maximum(along[None] * ratios[:, None, None] - 1.0, 0.0)
    return density + time_step * (quad + growth * density)


def inflow(ratios, inv_area, delta_x, delta_y):
    cosine, sine = direction_tables()
    speeds = group_scale / ratios
    facing = -(cosine[:, None] * delta_x[None, :] + sine[:, None] * delta_y[None, :])
    return (time_step * speeds)[:, None, None] * jnp.maximum(facing, 0.0)[None] * inv_area[None, None, :]


def reference(spectra, coords, inv_area, wind_vector, neighbours, send_nodes, send_count):
    parts_count = NODES // NP
    node_ids = jnp.arange(NODES, dtype=jnp.int32)
    owner = node_ids // NP
    ratios = jnp.power(freq_ratio, (jnp.arange(NF, dtype=jnp.int32) - NF // 2).astype(jnp.float32))
    widened = jnp.pad(spectra, ((REACH, REACH), (0, 0), (0, 0)))
    base = source_terms(spectra, widened, ratios, wind_vector)
    targets = []
    valids = []
    for slot_index in range(K):
        entry = neighbours[slot_index]
        is_local = entry < NP
        ghost = jnp.maximum(entry - NP, 0)
        source = ghost // CAP
        place = ghost % CAP
        pair = source * parts_count + owner
        remote = source * NP + send_nodes[pair, place]
        alive = place < send_count[pair]
        targets.append(jnp.where(is_local, owner * NP + entry, remote).astype(jnp.int32))
        valids.append(jnp.logical_or(is_local, alive).astype(jnp.float32))
    current = spectra
    for sweep_num in range(SWEEPS):
        total = base
        weight_sum = jnp.ones_like(spectra)
        for slot_index in range(K):
            target = targets[slot_index]
            valid = valids[slot_index]
            delta_x = coords[0][target] * valid - coords[0]
            delta_y = coords[1][target] * valid - coords[1]
            weights = inflow(ratios, inv_area, delta_x, delta_y)
            total = total + weights * (jnp.take(current, target, axis=2) * valid[None, None, :])
            weight_sum = weight_sum + weights
        current = total / weight_sum
    return current
```

```python
import math

import jax
import jax.numpy as jnp
import numpy as np
from jax import lax
from jax.experimental import pallas as pl
from jax.experimental.pallas import tpu as pltpu
from jax.sharding import PartitionSpec as P

NF = 36
ND = 36
K = 8
NP = 512
CAP = 8
N_MESH = 32
GHOSTS = N_MESH * CAP
BAND = 9
UP_REACH = 2
DOWN_REACH = 3
UP_SHIFT = 1
DOWN_SHIFT = 3
STRIDE = 40
ROWS = BAND * STRIDE + 8
LANES = 384

time_step = 0.5
group_scale = 0.8
quad_coupling = 0.25
wind_growth = 0.1
RATIOS = np.power(np.float64(1.1), np.arange(NF) - NF // 2)


def bf16_pieces(x):
    high = x.astype(jnp.bfloat16)
    low = (x - high.astype(jnp.float32)).astype(jnp.bfloat16)
    return jnp.concatenate([high, low], axis=0)


def exact_rows(c):
    high = c.astype(jnp.bfloat16).astype(jnp.float32)
    mid = (c - high).astype(jnp.bfloat16).astype(jnp.float32)
    return high + mid, (c - high) - mid


def by_band(band, values):
    picked = jnp.float32(values[3])
    for index in (2, 1, 0):
        picked = jnp.where(band == index, jnp.float32(values[index]), picked)
    return picked


def ratio_of(band, f):
    return by_band(band, [RATIOS[b * BAND + f] for b in range(NF // BAND)])


def scale_of(band, f):
    return by_band(band, [time_step * group_scale / RATIOS[b * BAND + f] for b in range(NF // BAND)])


def one_hot(entry_row, first, count):
    node = lax.broadcasted_iota(jnp.int32, (count, entry_row.shape[1]), 0) + first
    return jnp.where(node == entry_row, 1.0, 0.0).astype(jnp.bfloat16)


def gather(pieces, entry_row, first):
    got = jnp.dot(pieces, one_hot(entry_row, first, pieces.shape[1]), preferred_element_type=jnp.float32)
    return got[:ROWS] + got[ROWS:]


def fill_rows(rows_ref, planes, coords):
    rows_ref[...] = jnp.zeros_like(rows_ref)
    for f in range(BAND):
        rows_ref[f * STRIDE : f * STRIDE + ND, :] = planes[f]
    if coords is not None:
        base = BAND * STRIDE
        for axis in range(2):
            first, second = exact_rows(coords[axis : axis + 1, :])
            rows_ref[base + 2 * axis : base + 2 * axis + 1, :] = first
            rows_ref[base + 2 * axis + 1 : base + 2 * axis + 2, :] = second


def pack(pieces, send_ref, count_ref):
    slots = jnp.concatenate([send_ref[...].astype(jnp.float32)] * N_MESH, axis=0)
    counts = jnp.broadcast_to(count_ref[...].astype(jnp.float32), slots.shape)
    row = lax.broadcasted_iota(jnp.int32, slots.shape, 0)
    mine = lax.broadcasted_iota(jnp.int32, slots.shape, 1) == row // CAP
    node = jnp.sum(jnp.where(mine, slots, 0.0), axis=1, keepdims=True)
    count = jnp.sum(jnp.where(mine, counts, 0.0), axis=1, keepdims=True)
    place = lax.broadcasted_iota(jnp.int32, (GHOSTS, 1), 0) % CAP
    node = jnp.where(place.astype(jnp.float32) < count, node, -1.0).astype(jnp.int32)
    hot = jnp.where(lax.broadcasted_iota(jnp.int32, (GHOSTS, NP), 1) == node, 1.0, 0.0).astype(jnp.bfloat16)
    dims = (((1,), (1,)), ((), ()))
    return lax.dot_general(hot, pieces[:ROWS], dims, preferred_element_type=jnp.float32) + lax.dot_general(
        hot, pieces[ROWS:], dims, preferred_element_type=jnp.float32
    )


def wide(table):
    return jnp.concatenate([table] * (NP // 128), axis=1)


def pack_kernel(spectra_ref, coords_ref, send_ref, count_ref, out_ref, rows_ref):
    fill_rows(rows_ref, [spectra_ref[f] for f in range(BAND)], coords_ref[...])
    out_ref[:, :ROWS] = pack(bf16_pieces(rows_ref[...]), send_ref, count_ref)
    out_ref[:, ROWS:] = jnp.zeros((GHOSTS, LANES - ROWS), jnp.float32)


def facing(cosine, sine, coords, got):
    base = BAND * STRIDE
    delta_x = (got[base : base + 1] + got[base + 1 : base + 2]) - coords[0:1]
    delta_y = (got[base + 2 : base + 3] + got[base + 3 : base + 4]) - coords[1:2]
    return jnp.maximum(-(cosine * delta_x + sine * delta_y), 0.0)


def rolled(x, shift):
    shift = shift % ND
    return jnp.concatenate([x[ND - shift :], x[: ND - shift]], axis=0)


def local_kernel(
    band_ref, spectra_ref, lower_ref, upper_ref, coords_ref, wind_ref, near_ref, table_ref,
    base_ref, partial_ref, inflow_ref, rows_ref,
):
    band = band_ref[0]
    coords = coords_ref[...]
    fill_rows(rows_ref, [spectra_ref[f] for f in range(BAND)], coords)
    pieces = bf16_pieces(rows_ref[...])
    cosine, sine = wide(table_ref[0])[:ND], wide(table_ref[1])[:ND]
    for k in range(K):
        entry = near_ref[k : k + 1, :]
        got = gather(pieces, entry, 0)
        inflow = jnp.where(entry < NP, facing(cosine, sine, coords, got), 0.0)
        inflow_ref[k] = inflow
        for f in range(BAND):
            term = inflow * got[f * STRIDE : f * STRIDE + ND]
            partial_ref[f] = term if k == 0 else partial_ref[f] + term
    along = cosine * wind_ref[0:1, :] + sine * wind_ref[1:2, :]
    for f in range(BAND):
        density = spectra_ref[f]
        up = spectra_ref[f + UP_REACH] if f + UP_REACH < BAND else upper_ref[f + UP_REACH - BAND]
        down = spectra_ref[f - DOWN_REACH] if f >= DOWN_REACH else lower_ref[f]
        up_left, up_right = rolled(up, -UP_SHIFT), rolled(up, UP_SHIFT)
        down_left, down_right = rolled(down, DOWN_SHIFT), rolled(down, -DOWN_SHIFT)
        quad = quad_coupling * (
            density * density * (up_left + down_left + up_right + down_right)
            - 2.0 * density * (up_left * down_left + up_right * down_right)
        )
        growth = wind_growth * jnp.maximum(ratio_of(band, f) * along - 1.0, 0.0)
        base_ref[f] = density + time_step * (quad + growth * density)


def settle(band, f, base, area, total, weight):
    scaled = scale_of(band, f) * area
    return (base + scaled * total) / (1.0 + scaled * weight)


def ghost_pieces(ghost_ref):
    return bf16_pieces(ghost_ref[...].T[:ROWS])


def first_kernel(
    band_ref, ghost_ref, base_ref, partial_ref, inflow_ref, coords_ref, area_ref, near_ref, send_ref, count_ref, table_ref,
    packed_ref, pieces_ref, inflow_out_ref, weight_ref, total_ref, rows_ref,
):
    band = band_ref[0]
    coords = coords_ref[...]
    pieces = ghost_pieces(ghost_ref)
    cosine, sine = wide(table_ref[0])[:ND], wide(table_ref[1])[:ND]
    weight = jnp.zeros((ND, NP), jnp.float32)
    for k in range(K):
        entry = near_ref[k : k + 1, :]
        got = gather(pieces, entry, NP)
        inflow = jnp.where(entry < NP, 0.0, facing(cosine, sine, coords, got))
        both = inflow_ref[k] + inflow
        inflow_out_ref[k] = both
        weight = weight + both
        for f in range(BAND):
            term = inflow * got[f * STRIDE : f * STRIDE + ND]
            total_ref[f] = (partial_ref[f] if k == 0 else total_ref[f]) + term
    weight_ref[...] = weight
    area = area_ref[...]
    fill_rows(rows_ref, [settle(band, f, base_ref[f], area, total_ref[f], weight) for f in range(BAND)], None)
    pieces = bf16_pieces(rows_ref[...])
    pieces_ref[...] = pieces
    packed_ref[:, :ROWS] = pack(pieces, send_ref, count_ref)
    packed_ref[:, ROWS:] = jnp.zeros((GHOSTS, LANES - ROWS), jnp.float32)


def second_local_kernel(pieces_ref, inflow_ref, near_ref, partial_ref):
    pieces = pieces_ref[...]
    for k in range(K):
        got = gather(pieces, near_ref[k : k + 1, :], 0)
        for f in range(BAND):
            term = inflow_ref[k] * got[f * STRIDE : f * STRIDE + ND]
            partial_ref[f] = term if k == 0 else partial_ref[f] + term


def second_kernel(
    band_ref, ghost_ref, base_ref, partial_ref, inflow_ref, weight_ref, area_ref, near_ref, out_ref, total_ref
):
    band = band_ref[0]
    pieces = ghost_pieces(ghost_ref)
    for k in range(K):
        got = gather(pieces, near_ref[k : k + 1, :], NP)
        for f in range(BAND):
            term = inflow_ref[k] * got[f * STRIDE : f * STRIDE + ND]
            total_ref[f] = (partial_ref[f] if k == 0 else total_ref[f]) + term
    area, weight = area_ref[...], weight_ref[...]
    for f in range(BAND):
        out_ref[f] = settle(band, f, base_ref[f], area, total_ref[f], weight)


def call(kernel, outs, scratch, name, scalars, *operands):
    vmem, smem = pl.BlockSpec(memory_space=pltpu.VMEM), pl.BlockSpec(memory_space=pltpu.SMEM)
    return pl.pallas_call(
        kernel,
        out_shape=[jax.ShapeDtypeStruct(shape, dtype) for shape, dtype in outs],
        in_specs=[smem] * len(scalars) + [vmem] * len(operands),
        out_specs=[vmem] * len(outs),
        scratch_shapes=[pltpu.VMEM(shape, jnp.float32) for shape in scratch],
        compiler_params=pltpu.CompilerParams(vmem_limit_bytes=48 << 20),
        name=name,
    )(*scalars, *operands)


def local(spectra, coords, inv_area, wind_vector, neighbours, send_nodes, send_count):
    bands = lax.axis_size("freq")
    band = lax.axis_index("freq").astype(jnp.int32).reshape(1)
    ends = bands - 1
    lower = lax.ppermute(spectra[BAND - DOWN_REACH :], "freq", [(i, i + 1) for i in range(ends)])
    upper = lax.ppermute(spectra[:UP_REACH], "freq", [(i + 1, i) for i in range(ends)])
    angles = (np.arange(STRIDE) + 0.5) * (2.0 * math.pi / ND)
    table = jnp.asarray(
        np.broadcast_to(np.stack([np.cos(angles), np.sin(angles)])[:, :, None], (2, STRIDE, 128)), jnp.float32
    )
    send, count, area = send_nodes.T, send_count.reshape(1, -1), inv_area.reshape(1, -1)
    f32, planes = jnp.float32, (BAND, ND, NP)

    def exchange(packed):
        packed = packed.reshape(N_MESH, CAP, LANES)
        return lax.all_to_all(packed, "mesh", split_axis=0, concat_axis=0, tiled=True).reshape(GHOSTS, LANES)

    (packed,) = call(
        pack_kernel, [((GHOSTS, LANES), f32)], [(ROWS, NP)], "pack", (), spectra, coords, send, count
    )
    ghosts = exchange(packed)
    base, partial, inflow = call(
        local_kernel, [(planes, f32), (planes, f32), ((K, ND, NP), f32)], [(ROWS, NP)], "local_first",
        (band,), spectra, lower, upper, coords, wind_vector, neighbours, table,
    )
    packed, pieces, inflow, weight = call(
        first_kernel,
        [((GHOSTS, LANES), f32), ((2 * ROWS, NP), jnp.bfloat16), ((K, ND, NP), f32), ((ND, NP), f32)],
        [planes, (ROWS, NP)], "first",
        (band,), ghosts, base, partial, inflow, coords, area, neighbours, send, count, table,
    )
    ghosts = exchange(packed)
    (partial,) = call(second_local_kernel, [(planes, f32)], [], "local_second", (), pieces, inflow, neighbours)
    (updated,) = call(
        second_kernel, [(planes, f32)], [planes], "second",
        (band,), ghosts, base, partial, inflow, weight, area, neighbours,
    )
    return updated


def solution(mesh):
    in_specs = (
        P("freq", None, "mesh"),
        P(None, "mesh"),
        P("mesh"),
        P(None, "mesh"),
        P(None, "mesh"),
        P("mesh", None),
        P("mesh"),
    )
    out_specs = P("freq", None, "mesh")
    return jax.shard_map(local, mesh=mesh, in_specs=in_specs, out_specs=out_specs, check_vma=False)
```

```python
import math

import jax
import jax.numpy as jnp
import numpy as np
from jax import lax
from jax.experimental import pallas as pl
from jax.experimental.pallas import tpu as pltpu
from jax.sharding import PartitionSpec as P

NF = 36
ND = 36
K = 8
NP = 512
CAP = 8
N_MESH = 32
GHOSTS = N_MESH * CAP
BAND = 9
UP_REACH = 2
DOWN_REACH = 3
UP_SHIFT = 1
DOWN_SHIFT = 3
STRIDE = 40
ROWS = BAND * STRIDE + 8
LANES = 384

time_step = 0.5
group_scale = 0.8
quad_coupling = 0.25
wind_growth = 0.1
RATIOS = np.power(np.float64(1.1), np.arange(NF) - NF // 2)


def bf16_pieces(x):
    high = x.astype(jnp.bfloat16)
    low = (x - high.astype(jnp.float32)).astype(jnp.bfloat16)
    return jnp.concatenate([high, low], axis=0)


def exact_rows(c):
    high = c.astype(jnp.bfloat16).astype(jnp.float32)
    mid = (c - high).astype(jnp.bfloat16).astype(jnp.float32)
    return high + mid, (c - high) - mid


def by_band(band, values):
    picked = jnp.float32(values[3])
    for index in (2, 1, 0):
        picked = jnp.where(band == index, jnp.float32(values[index]), picked)
    return picked


def ratio_of(band, f):
    return by_band(band, [RATIOS[b * BAND + f] for b in range(NF // BAND)])


def scale_of(band, f):
    return by_band(band, [time_step * group_scale / RATIOS[b * BAND + f] for b in range(NF // BAND)])


def one_hot(entry_row, first, count):
    node = lax.broadcasted_iota(jnp.int32, (count, entry_row.shape[1]), 0) + first
    return jnp.where(node == entry_row, 1.0, 0.0).astype(jnp.bfloat16)


def gather(pieces, entry_row, first):
    got = jnp.dot(pieces, one_hot(entry_row, first, pieces.shape[1]), preferred_element_type=jnp.float32)
    return got[:ROWS] + got[ROWS:]


def fill_rows(rows_ref, planes, coords):
    rows_ref[...] = jnp.zeros_like(rows_ref)
    for f in range(BAND):
        rows_ref[f * STRIDE : f * STRIDE + ND, :] = planes[f]
    if coords is not None:
        base = BAND * STRIDE
        for axis in range(2):
            first, second = exact_rows(coords[axis : axis + 1, :])
            rows_ref[base + 2 * axis : base + 2 * axis + 1, :] = first
            rows_ref[base + 2 * axis + 1 : base + 2 * axis + 2, :] = second


def pack(pieces, send_ref, count_ref):
    slots = jnp.concatenate([send_ref[...].astype(jnp.float32)] * N_MESH, axis=0)
    counts = jnp.broadcast_to(count_ref[...].astype(jnp.float32), slots.shape)
    row = lax.broadcasted_iota(jnp.int32, slots.shape, 0)
    mine = lax.broadcasted_iota(jnp.int32, slots.shape, 1) == row // CAP
    node = jnp.sum(jnp.where(mine, slots, 0.0), axis=1, keepdims=True)
    count = jnp.sum(jnp.where(mine, counts, 0.0), axis=1, keepdims=True)
    place = lax.broadcasted_iota(jnp.int32, (GHOSTS, 1), 0) % CAP
    node = jnp.where(place.astype(jnp.float32) < count, node, -1.0).astype(jnp.int32)
    hot = jnp.where(lax.broadcasted_iota(jnp.int32, (GHOSTS, NP), 1) == node, 1.0, 0.0).astype(jnp.bfloat16)
    dims = (((1,), (1,)), ((), ()))
    return lax.dot_general(hot, pieces[:ROWS], dims, preferred_element_type=jnp.float32) + lax.dot_general(
        hot, pieces[ROWS:], dims, preferred_element_type=jnp.float32
    )


def wide(table):
    return jnp.concatenate([table] * (NP // 128), axis=1)


def pack_kernel(*refs):
    sources, out_ref, rows_ref, buffers, sems = refs[:4], refs[4], refs[5], refs[6:10], refs[10]
    copies = [pltpu.make_async_copy(sources[i], buffers[i], sems.at[i]) for i in range(4)]
    for copy in copies:
        copy.start()
    for copy in copies:
        copy.wait()
    spectra_ref, coords_ref, send_ref, count_ref = buffers
    fill_rows(rows_ref, [spectra_ref[f] for f in range(BAND)], coords_ref[...])
    out_ref[:, :ROWS] = pack(bf16_pieces(rows_ref[...]), send_ref, count_ref)
    out_ref[:, ROWS:] = jnp.zeros((GHOSTS, LANES - ROWS), jnp.float32)


def delta(got, coords, axis):
    base = BAND * STRIDE + 2 * axis
    return (got[base : base + 1] + got[base + 1 : base + 2]) - coords[axis : axis + 1]


def facing(cosine, sine, delta_x, delta_y):
    return jnp.maximum(-(cosine * delta_x + sine * delta_y), 0.0)


def rolled(x, shift):
    shift = shift % ND
    return jnp.concatenate([x[ND - shift :], x[: ND - shift]], axis=0)


def local_kernel(
    band_ref, spectra_ref, lower_ref, upper_ref, coords_ref, wind_ref, area_ref, near_ref, table_ref,
    base_ref, partial_ref, rows_ref,
):
    band = band_ref[0]
    coords = coords_ref[...]
    fill_rows(rows_ref, [spectra_ref[f] for f in range(BAND)], coords)
    pieces = bf16_pieces(rows_ref[...])
    cosine, sine = wide(table_ref[0])[:ND], wide(table_ref[1])[:ND]
    for k in range(K):
        entry = near_ref[k : k + 1, :]
        got = gather(pieces, entry, 0)
        delta_x = jnp.where(entry < NP, delta(got, coords, 0), 0.0)
        delta_y = jnp.where(entry < NP, delta(got, coords, 1), 0.0)
        partial_ref[k, ND : ND + 1] = delta_x
        partial_ref[k, ND + 1 : ND + 2] = delta_y
        inflow = facing(cosine, sine, delta_x, delta_y)
        for f in range(BAND):
            term = inflow * got[f * STRIDE : f * STRIDE + ND]
            partial_ref[f, :ND] = term if k == 0 else partial_ref[f, :ND] + term
    partial_ref[K, ND : ND + 1] = area_ref[...]
    along = cosine * wind_ref[0:1, :] + sine * wind_ref[1:2, :]
    for f in range(BAND):
        density = spectra_ref[f]
        up = spectra_ref[f + UP_REACH] if f + UP_REACH < BAND else upper_ref[f + UP_REACH - BAND]
        down = spectra_ref[f - DOWN_REACH] if f >= DOWN_REACH else lower_ref[f]
        up_left, up_right = rolled(up, -UP_SHIFT), rolled(up, UP_SHIFT)
        down_left, down_right = rolled(down, DOWN_SHIFT), rolled(down, -DOWN_SHIFT)
        quad = quad_coupling * (
            density * density * (up_left + down_left + up_right + down_right)
            - 2.0 * density * (up_left * down_left + up_right * down_right)
        )
        growth = wind_growth * jnp.maximum(ratio_of(band, f) * along - 1.0, 0.0)
        base_ref[f] = density + time_step * (quad + growth * density)


def settle(band, f, base, area, total, weight):
    scaled = scale_of(band, f) * area
    return (base + scaled * total) / (1.0 + scaled * weight)


def ghost_pieces(ghost_ref):
    return bf16_pieces(ghost_ref[...].T[:ROWS])


def first_kernel(
    band_ref, ghost_ref, base_ref, partial_ref, coords_ref, near_ref, send_ref, count_ref, table_ref,
    packed_ref, pieces_ref, delta_ref, total_ref, rows_ref,
):
    band = band_ref[0]
    coords = coords_ref[...]
    pieces = ghost_pieces(ghost_ref)
    cosine, sine = wide(table_ref[0])[:ND], wide(table_ref[1])[:ND]
    weight = jnp.zeros((ND, NP), jnp.float32)
    for k in range(K):
        entry = near_ref[k : k + 1, :]
        got = gather(pieces, entry, NP)
        delta_x = jnp.where(entry < NP, partial_ref[k, ND : ND + 1], delta(got, coords, 0))
        delta_y = jnp.where(entry < NP, partial_ref[k, ND + 1 : ND + 2], delta(got, coords, 1))
        delta_ref[k : k + 1, :] = delta_x
        delta_ref[K + k : K + k + 1, :] = delta_y
        inflow = facing(cosine, sine, delta_x, delta_y)
        weight = weight + inflow
        for f in range(BAND):
            term = inflow * got[f * STRIDE : f * STRIDE + ND]
            total_ref[f] = (partial_ref[f, :ND] if k == 0 else total_ref[f]) + term
    area = partial_ref[K, ND : ND + 1]
    delta_ref[2 * K : 2 * K + 1, :] = area
    fill_rows(rows_ref, [settle(band, f, base_ref[f], area, total_ref[f], weight) for f in range(BAND)], None)
    pieces = bf16_pieces(rows_ref[...])
    pieces_ref[...] = pieces
    packed_ref[:, :ROWS] = pack(pieces, send_ref, count_ref)
    packed_ref[:, ROWS:] = jnp.zeros((GHOSTS, LANES - ROWS), jnp.float32)


def second_local_kernel(pieces_ref, delta_ref, near_ref, table_ref, partial_ref):
    pieces = pieces_ref[...]
    cosine, sine = wide(table_ref[0])[:ND], wide(table_ref[1])[:ND]
    for k in range(K):
        got = gather(pieces, near_ref[k : k + 1, :], 0)
        inflow = facing(cosine, sine, delta_ref[k : k + 1, :], delta_ref[K + k : K + k + 1, :])
        for f in range(BAND):
            term = inflow * got[f * STRIDE : f * STRIDE + ND]
            partial_ref[f] = term if k == 0 else partial_ref[f] + term


def second_kernel(
    band_ref, ghost_ref, base_ref, partial_ref, delta_ref, near_ref, table_ref, out_ref, total_ref
):
    band = band_ref[0]
    pieces = ghost_pieces(ghost_ref)
    cosine, sine = wide(table_ref[0])[:ND], wide(table_ref[1])[:ND]
    weight = jnp.zeros((ND, NP), jnp.float32)
    for k in range(K):
        got = gather(pieces, near_ref[k : k + 1, :], NP)
        inflow = facing(cosine, sine, delta_ref[k : k + 1, :], delta_ref[K + k : K + k + 1, :])
        weight = weight + inflow
        for f in range(BAND):
            term = inflow * got[f * STRIDE : f * STRIDE + ND]
            total_ref[f] = (partial_ref[f] if k == 0 else total_ref[f]) + term
    area = delta_ref[2 * K : 2 * K + 1, :]
    for f in range(BAND):
        out_ref[f] = settle(band, f, base_ref[f], area, total_ref[f], weight)


def call(kernel, outs, scratch, name, scalars, *operands):
    vmem, smem = pl.BlockSpec(memory_space=pltpu.VMEM), pl.BlockSpec(memory_space=pltpu.SMEM)
    return pl.pallas_call(
        kernel,
        out_shape=[jax.ShapeDtypeStruct(shape, dtype) for shape, dtype in outs],
        in_specs=[smem] * len(scalars) + [vmem] * len(operands),
        out_specs=[vmem] * len(outs),
        scratch_shapes=[pltpu.VMEM(shape, jnp.float32) for shape in scratch],
        compiler_params=pltpu.CompilerParams(vmem_limit_bytes=24 << 20),
        name=name,
    )(*scalars, *operands)


def local(spectra, coords, inv_area, wind_vector, neighbours, send_nodes, send_count):
    bands = lax.axis_size("freq")
    band = lax.axis_index("freq").astype(jnp.int32).reshape(1)
    ends = bands - 1
    lower = lax.ppermute(spectra[BAND - DOWN_REACH :], "freq", [(i, i + 1) for i in range(ends)])
    upper = lax.ppermute(spectra[:UP_REACH], "freq", [(i + 1, i) for i in range(ends)])
    angles = (np.arange(STRIDE) + 0.5) * (2.0 * math.pi / ND)
    table = jnp.asarray(
        np.broadcast_to(np.stack([np.cos(angles), np.sin(angles)])[:, :, None], (2, STRIDE, 128)), jnp.float32
    )
    send, count, area = send_nodes.T, send_count.reshape(1, -1), inv_area.reshape(1, -1)
    f32, planes = jnp.float32, (BAND, ND, NP)

    def exchange(packed):
        packed = packed.reshape(N_MESH, CAP, LANES)
        return lax.all_to_all(packed, "mesh", split_axis=0, concat_axis=0, tiled=True).reshape(GHOSTS, LANES)

    inputs = (spectra, coords, send, count)
    packed = pl.pallas_call(
        pack_kernel,
        out_shape=jax.ShapeDtypeStruct((GHOSTS, LANES), f32),
        in_specs=[pl.BlockSpec(memory_space=pltpu.HBM)] * len(inputs),
        out_specs=pl.BlockSpec(memory_space=pltpu.VMEM),
        scratch_shapes=[
            pltpu.VMEM((ROWS, NP), f32),
            *[pltpu.VMEM(x.shape, x.dtype) for x in inputs],
            pltpu.SemaphoreType.DMA((len(inputs),)),
        ],
        compiler_params=pltpu.CompilerParams(vmem_limit_bytes=24 << 20),
        name="pack",
    )(*inputs)
    packed, lower, upper = lax.optimization_barrier((packed, lower, upper))
    ghosts = exchange(packed)
    base, partial = call(
        local_kernel, [(planes, f32), ((BAND, STRIDE, NP), f32)], [(ROWS, NP)], "local_first",
        (band,), spectra, lower, upper, coords, wind_vector, area, neighbours, table,
    )
    packed, pieces, deltas = call(
        first_kernel,
        [((GHOSTS, LANES), f32), ((2 * ROWS, NP), jnp.bfloat16), ((3 * K, NP), f32)],
        [planes, (ROWS, NP)], "first",
        (band,), ghosts, base, partial, coords, neighbours, send, count, table,
    )
    ghosts = exchange(packed)
    (partial,) = call(second_local_kernel, [(planes, f32)], [], "local_second", (), pieces, deltas, neighbours, table)
    (updated,) = call(
        second_kernel, [(planes, f32)], [planes], "second",
        (band,), ghosts, base, partial, deltas, neighbours, table,
    )
    return updated


def solution(mesh):
    in_specs = (
        P("freq", None, "mesh"),
        P(None, "mesh"),
        P("mesh"),
        P(None, "mesh"),
        P(None, "mesh"),
        P("mesh", None),
        P("mesh"),
    )
    out_specs = P("freq", None, "mesh")
    return jax.shard_map(local, mesh=mesh, in_specs=in_specs, out_specs=out_specs, check_vma=False)
```

```python
import math

import jax
import jax.numpy as jnp
import numpy as np
from jax import lax
from jax.experimental import pallas as pl
from jax.experimental.pallas import tpu as pltpu
from jax.sharding import PartitionSpec as P

NF = 36
ND = 36
K = 8
NP = 512
CAP = 8
N_MESH = 32
GHOSTS = N_MESH * CAP
BAND = 9
UP_REACH = 2
DOWN_REACH = 3
UP_SHIFT = 1
DOWN_SHIFT = 3
STRIDE = 40
ROWS = BAND * STRIDE + 8
LANES = 384

time_step = 0.5
group_scale = 0.8
quad_coupling = 0.25
wind_growth = 0.1
RATIOS = np.power(np.float64(1.1), np.arange(NF) - NF // 2)


def bf16_pieces(x):
    high = x.astype(jnp.bfloat16)
    low = (x - high.astype(jnp.float32)).astype(jnp.bfloat16)
    return jnp.concatenate([high, low], axis=0)


def exact_rows(c):
    high = c.astype(jnp.bfloat16).astype(jnp.float32)
    mid = (c - high).astype(jnp.bfloat16).astype(jnp.float32)
    return high + mid, (c - high) - mid


def by_band(band, values):
    picked = jnp.float32(values[3])
    for index in (2, 1, 0):
        picked = jnp.where(band == index, jnp.float32(values[index]), picked)
    return picked


def ratio_of(band, f):
    return by_band(band, [RATIOS[b * BAND + f] for b in range(NF // BAND)])


def scale_of(band, f):
    return by_band(band, [time_step * group_scale / RATIOS[b * BAND + f] for b in range(NF // BAND)])


def one_hot(entry_row, first, count):
    node = lax.broadcasted_iota(jnp.int32, (count, entry_row.shape[1]), 0) + first
    return jnp.where(node == entry_row, 1.0, 0.0).astype(jnp.bfloat16)


def gather(pieces, entry_row, first):
    got = jnp.dot(pieces, one_hot(entry_row, first, pieces.shape[1]), preferred_element_type=jnp.float32)
    return got[:ROWS] + got[ROWS:]


HALF = NP // 2
BOTTOM = BAND * STRIDE


def fill_rows(rows_ref, planes, cols):
    for f in range(BAND):
        rows_ref[f * STRIDE : f * STRIDE + ND, cols] = planes[f]


def packing_one_hot(send, count):
    slots = jnp.concatenate([send.astype(jnp.float32)] * N_MESH, axis=0)
    counts = jnp.broadcast_to(count.astype(jnp.float32), slots.shape)
    row = lax.broadcasted_iota(jnp.int32, slots.shape, 0)
    mine = lax.broadcasted_iota(jnp.int32, slots.shape, 1) == row // CAP
    node = jnp.sum(jnp.where(mine, slots, 0.0), axis=1, keepdims=True)
    used = jnp.sum(jnp.where(mine, counts, 0.0), axis=1, keepdims=True)
    place = lax.broadcasted_iota(jnp.int32, (GHOSTS, 1), 0) % CAP
    node = jnp.where(place.astype(jnp.float32) < used, node, -1.0).astype(jnp.int32)
    return jnp.where(lax.broadcasted_iota(jnp.int32, (GHOSTS, NP), 1) == node, 1.0, 0.0).astype(jnp.bfloat16)


def picked(hot, pieces):
    dims = (((1,), (1,)), ((), ()))
    return lax.dot_general(hot, pieces[:ROWS], dims, preferred_element_type=jnp.float32) + lax.dot_general(
        hot, pieces[ROWS:], dims, preferred_element_type=jnp.float32
    )


def wide(table, width):
    return jnp.concatenate([table] * (width // 128), axis=1)[:ND]


def delta(got, coords, axis):
    base = BOTTOM + 2 * axis
    return (got[base : base + 1] + got[base + 1 : base + 2]) - coords[axis : axis + 1]


def facing(cosine, sine, delta_x, delta_y):
    return jnp.maximum(-(cosine * delta_x + sine * delta_y), 0.0)


def rolled(x, shift):
    shift = shift % ND
    return jnp.concatenate([x[ND - shift :], x[: ND - shift]], axis=0)


def load_kernel(*refs):
    count = (len(refs) - 3) // 2
    sources, targets, sems = list(refs[:count]), refs[count:-1], refs[-1]
    sources += [
        sources[0].at[pl.ds(BAND - DOWN_REACH, DOWN_REACH)],
        sources[0].at[pl.ds(0, UP_REACH)],
    ]
    copies = [pltpu.make_async_copy(source, target, sems.at[i]) for i, (source, target) in enumerate(zip(sources, targets))]
    for copy in copies:
        copy.start()
    for copy in copies:
        copy.wait()


def spectra_pieces(spectra_ref, coords_ref, rows_ref):
    rows_ref[...] = jnp.zeros_like(rows_ref)
    for axis in range(2):
        first, second = exact_rows(coords_ref[axis : axis + 1, :])
        rows_ref[BOTTOM + 2 * axis : BOTTOM + 2 * axis + 1, :] = first
        rows_ref[BOTTOM + 2 * axis + 1 : BOTTOM + 2 * axis + 2, :] = second
    fill_rows(rows_ref, [spectra_ref[f] for f in range(BAND)], slice(None))
    return bf16_pieces(rows_ref[...])


def pack_kernel(spectra_ref, coords_ref, send_ref, count_ref, packed_ref, rows_ref):
    pieces = spectra_pieces(spectra_ref, coords_ref, rows_ref)
    packed_ref[:, :ROWS] = picked(packing_one_hot(send_ref[...], count_ref[...]), pieces)
    packed_ref[:, ROWS:] = jnp.zeros((GHOSTS, LANES - ROWS), jnp.float32)


def local_kernel(
    band_ref, spectra_ref, lower_ref, upper_ref, coords_ref, wind_ref, area_ref, near_ref, table_ref,
    base_ref, partial_ref, rows_ref,
):
    band = band_ref[0]
    pieces = spectra_pieces(spectra_ref, coords_ref, rows_ref)
    cosine, sine = wide(table_ref[0], NP), wide(table_ref[1], NP)
    for k in range(K):
        entry = near_ref[k : k + 1, :]
        got = gather(pieces, entry, 0)
        delta_x = jnp.where(entry < NP, delta(got, coords_ref[...], 0), 0.0)
        delta_y = jnp.where(entry < NP, delta(got, coords_ref[...], 1), 0.0)
        partial_ref[k, ND : ND + 1] = delta_x
        partial_ref[k, ND + 1 : ND + 2] = delta_y
        inflow = facing(cosine, sine, delta_x, delta_y)
        for f in range(BAND):
            term = inflow * got[f * STRIDE : f * STRIDE + ND]
            partial_ref[f, :ND] = term if k == 0 else partial_ref[f, :ND] + term
    partial_ref[K, ND : ND + 1] = area_ref[...]
    along = cosine * wind_ref[0:1, :] + sine * wind_ref[1:2, :]
    for f in range(BAND):
        density = spectra_ref[f]
        up = spectra_ref[f + UP_REACH] if f + UP_REACH < BAND else upper_ref[f + UP_REACH - BAND]
        down = spectra_ref[f - DOWN_REACH] if f >= DOWN_REACH else lower_ref[f]
        up_left, up_right = rolled(up, -UP_SHIFT), rolled(up, UP_SHIFT)
        down_left, down_right = rolled(down, DOWN_SHIFT), rolled(down, -DOWN_SHIFT)
        quad = quad_coupling * (
            density * density * (up_left + down_left + up_right + down_right)
            - 2.0 * density * (up_left * down_left + up_right * down_right)
        )
        growth = wind_growth * jnp.maximum(ratio_of(band, f) * along - 1.0, 0.0)
        base_ref[f] = density + time_step * (quad + growth * density)


def settle(band, f, base, area, total, weight):
    scaled = scale_of(band, f) * area
    return (base + scaled * total) / (1.0 + scaled * weight)


def ghost_pieces(ghost_ref):
    return bf16_pieces(ghost_ref[...].T[:ROWS])


def first_kernel(
    band_ref, ghost_ref, base_ref, partial_ref, coords_ref, near_ref, send_ref, count_ref, table_ref,
    packed_ref, pieces_ref, delta_ref, total_ref, rows_ref,
):
    band = band_ref[0]
    coords = coords_ref[...]
    pieces = ghost_pieces(ghost_ref)
    cosine, sine = wide(table_ref[0], NP), wide(table_ref[1], NP)
    weight = jnp.zeros((ND, NP), jnp.float32)
    for k in range(K):
        entry = near_ref[k : k + 1, :]
        got = gather(pieces, entry, NP)
        delta_x = jnp.where(entry < NP, partial_ref[k, ND : ND + 1], delta(got, coords, 0))
        delta_y = jnp.where(entry < NP, partial_ref[k, ND + 1 : ND + 2], delta(got, coords, 1))
        delta_ref[k : k + 1, :] = delta_x
        delta_ref[K + k : K + k + 1, :] = delta_y
        inflow = facing(cosine, sine, delta_x, delta_y)
        weight = weight + inflow
        for f in range(BAND):
            term = inflow * got[f * STRIDE : f * STRIDE + ND]
            total_ref[f] = (partial_ref[f, :ND] if k == 0 else total_ref[f]) + term
    area = partial_ref[K, ND : ND + 1]
    delta_ref[2 * K : 2 * K + 1, :] = area
    rows_ref[...] = jnp.zeros_like(rows_ref)
    fill_rows(rows_ref, [settle(band, f, base_ref[f], area, total_ref[f], weight) for f in range(BAND)], slice(None))
    current = bf16_pieces(rows_ref[...])
    pieces_ref[...] = current
    packed_ref[:, :ROWS] = picked(packing_one_hot(send_ref[...], count_ref[...]), current)
    packed_ref[:, ROWS:] = jnp.zeros((GHOSTS, LANES - ROWS), jnp.float32)


def second_local_kernel(pieces_ref, delta_ref, near_ref, table_ref, partial_ref):
    pieces = pieces_ref[...]
    cosine, sine = wide(table_ref[0], NP), wide(table_ref[1], NP)
    for k in range(K):
        got = gather(pieces, near_ref[k : k + 1, :], 0)
        inflow = facing(cosine, sine, delta_ref[k : k + 1, :], delta_ref[K + k : K + k + 1, :])
        for f in range(BAND):
            term = inflow * got[f * STRIDE : f * STRIDE + ND]
            partial_ref[f] = term if k == 0 else partial_ref[f] + term


def second_kernel(
    band_ref, ghost_ref, base_ref, partial_ref, delta_ref, near_ref, table_ref, out_ref, total_ref, sems
):
    band = band_ref[0]
    pieces = ghost_pieces(ghost_ref)
    cosine, sine = wide(table_ref[0], HALF), wide(table_ref[1], HALF)
    copies = []
    for half in range(2):
        cols = slice(half * HALF, (half + 1) * HALF)
        weight = jnp.zeros((ND, HALF), jnp.float32)
        for k in range(K):
            got = gather(pieces, near_ref[k : k + 1, cols], NP)
            inflow = facing(cosine, sine, delta_ref[k : k + 1, cols], delta_ref[K + k : K + k + 1, cols])
            weight = weight + inflow
            for f in range(BAND):
                term = inflow * got[f * STRIDE : f * STRIDE + ND]
                total_ref[f, :, cols] = (partial_ref[f, :, cols] if k == 0 else total_ref[f, :, cols]) + term
        area = delta_ref[2 * K : 2 * K + 1, cols]
        for f in range(BAND):
            total_ref[f, :, cols] = settle(band, f, base_ref[f, :, cols], area, total_ref[f, :, cols], weight)
        moved = pl.ds(half * HALF, HALF)
        copy = pltpu.make_async_copy(total_ref.at[:, :, moved], out_ref.at[:, :, moved], sems.at[half])
        copy.start()
        copies.append(copy)
    for copy in copies:
        copy.wait()


VMEM, SMEM, HBM = pltpu.VMEM, pltpu.SMEM, pltpu.HBM


def call(kernel, outs, scratch, name, *operands):
    return pl.pallas_call(
        kernel,
        out_shape=[jax.ShapeDtypeStruct(shape, dtype) for shape, dtype, _ in outs],
        in_specs=[pl.BlockSpec(memory_space=memory) for _, memory in operands],
        out_specs=[pl.BlockSpec(memory_space=memory) for _, _, memory in outs],
        scratch_shapes=scratch,
        compiler_params=pltpu.CompilerParams(vmem_limit_bytes=24 << 20),
        name=name,
        cost_estimate=pl.CostEstimate(flops=10**10, transcendentals=0, bytes_accessed=10**10),
    )(*[pltpu.with_memory_space_constraint(array, HBM) if memory is HBM else array for array, memory in operands])


def local(spectra, coords, inv_area, wind_vector, neighbours, send_nodes, send_count):
    bands = lax.axis_size("freq")
    band = lax.axis_index("freq").astype(jnp.int32).reshape(1)
    ends = bands - 1
    angles = (np.arange(STRIDE) + 0.5) * (2.0 * math.pi / ND)
    table = jnp.asarray(
        np.broadcast_to(np.stack([np.cos(angles), np.sin(angles)])[:, :, None], (2, STRIDE, 128)), jnp.float32
    )
    f32, planes = jnp.float32, (BAND, ND, NP)
    rows, dma = pltpu.VMEM((ROWS, NP), f32), pltpu.SemaphoreType.DMA
    split = ((2 * ROWS, NP), jnp.bfloat16, VMEM)

    def exchange(packed):
        packed = packed.reshape(N_MESH, CAP, LANES)
        return lax.all_to_all(packed, "mesh", split_axis=0, concat_axis=0, tiled=True).reshape(GHOSTS, LANES)

    def inside(*arrays):
        return [(array, VMEM) for array in arrays]

    inputs = (
        spectra, coords, wind_vector, inv_area.reshape(1, -1), neighbours,
        send_nodes.T, send_count.reshape(1, -1), table,
    )
    edges = [(DOWN_REACH, ND, NP), (UP_REACH, ND, NP)]
    spectra, coords, wind, area, near, send, count, table, tail, head = call(
        load_kernel,
        [(array.shape, array.dtype, VMEM) for array in inputs] + [(shape, f32, VMEM) for shape in edges],
        [dma((len(inputs) + 2,))],
        "load",
        *[(array, HBM) for array in inputs],
    )
    lower = lax.ppermute(tail, "freq", [(i, i + 1) for i in range(ends)])
    upper = lax.ppermute(head, "freq", [(i + 1, i) for i in range(ends)])
    (packed,) = call(
        pack_kernel, [((GHOSTS, LANES), f32, VMEM)], [rows], "pack", *inside(spectra, coords, send, count)
    )
    ghosts = exchange(packed)
    base, partial = call(
        local_kernel,
        [(planes, f32, VMEM), ((BAND, STRIDE, NP), f32, VMEM)],
        [rows],
        "local_first",
        (band, SMEM),
        *inside(spectra, lower, upper, coords, wind, area, near, table),
    )
    packed, pieces, deltas = call(
        first_kernel,
        [((GHOSTS, LANES), f32, VMEM), split, ((3 * K, NP), f32, VMEM)],
        [pltpu.VMEM(planes, f32), rows],
        "first",
        (band, SMEM),
        *inside(ghosts, base, partial, coords, near, send, count, table),
    )
    ghosts = exchange(packed)
    (partial,) = call(
        second_local_kernel, [(planes, f32, VMEM)], [], "local_second", *inside(pieces, deltas, near, table)
    )
    (updated,) = call(
        second_kernel,
        [(planes, f32, HBM)],
        [pltpu.VMEM(planes, f32), dma((2,))],
        "second",
        (band, SMEM),
        *inside(ghosts, base, partial, deltas, near, table),
    )
    return updated


def solution(mesh):
    in_specs = (
        P("freq", None, "mesh"),
        P(None, "mesh"),
        P("mesh"),
        P(None, "mesh"),
        P(None, "mesh"),
        P("mesh", None),
        P("mesh"),
    )
    out_specs = P("freq", None, "mesh")
    return jax.shard_map(local, mesh=mesh, in_specs=in_specs, out_specs=out_specs, check_vma=False)
```

```python
import math

import jax
import jax.numpy as jnp
import numpy as np
from jax import lax
from jax.experimental import pallas as pl
from jax.experimental.pallas import tpu as pltpu
from jax.sharding import PartitionSpec as P

NF = 36
ND = 36
K = 8
NP = 512
CAP = 8
N_MESH = 32
GHOSTS = N_MESH * CAP
BAND = 9
UP_REACH = 2
DOWN_REACH = 3
UP_SHIFT = 1
DOWN_SHIFT = 3
COORDS = BAND * ND
ROWS = COORDS + 4
LANES = 384
PAIR = 2 * ND
GROUPS = [(0, PAIR), (PAIR, PAIR), (2 * PAIR, PAIR), (3 * PAIR, PAIR), (4 * PAIR, ROWS - 4 * PAIR)]

time_step = 0.5
group_scale = 0.8
quad_coupling = 0.25
wind_growth = 0.1
RATIOS = np.power(np.float64(1.1), np.arange(NF) - NF // 2)


def rounded(x):
    return x.astype(jnp.bfloat16).astype(jnp.float32)


def bf16_pieces(x):
    high = rounded(x)
    return jnp.concatenate([high, x - high], axis=0).astype(jnp.bfloat16)


def exact_rows(c):
    high = rounded(c)
    mid = rounded(c - high)
    return high + mid, (c - high) - mid


def by_band(band, values):
    picked = jnp.float32(values[3])
    for index in (2, 1, 0):
        picked = jnp.where(band == index, jnp.float32(values[index]), picked)
    return picked


def ratio_of(band, f):
    return by_band(band, [RATIOS[b * BAND + f] for b in range(NF // BAND)])


def scale_of(band, f):
    return by_band(band, [time_step * group_scale / RATIOS[b * BAND + f] for b in range(NF // BAND)])


def one_hot(entry_row, first, count):
    node = lax.broadcasted_iota(jnp.int32, (count, entry_row.shape[1]), 0) + first
    return jnp.where(node == entry_row, 1.0, 0.0).astype(jnp.bfloat16)


def gather(pieces, entry_row, first):
    got = jnp.dot(pieces, one_hot(entry_row, first, pieces.shape[1]), preferred_element_type=jnp.float32)
    return got[:ROWS] + got[ROWS:]


def fill_coords(rows_ref, coords_ref):
    for axis in range(2):
        first, second = exact_rows(coords_ref[axis : axis + 1, :])
        rows_ref[COORDS + 2 * axis : COORDS + 2 * axis + 1, :] = first
        rows_ref[COORDS + 2 * axis + 1 : COORDS + 2 * axis + 2, :] = second


def fill_rows(rows_ref, spectra_ref, coords_ref):
    for f in range(BAND):
        rows_ref[f * ND : (f + 1) * ND, :] = spectra_ref[f]
    fill_coords(rows_ref, coords_ref)


def packing_one_hot(send, count):
    slots = jnp.concatenate([send.astype(jnp.float32)] * N_MESH, axis=0)
    counts = jnp.broadcast_to(count.astype(jnp.float32), slots.shape)
    row = lax.broadcasted_iota(jnp.int32, slots.shape, 0)
    mine = lax.broadcasted_iota(jnp.int32, slots.shape, 1) == row // CAP
    node = jnp.sum(jnp.where(mine, slots, 0.0), axis=1, keepdims=True)
    used = jnp.sum(jnp.where(mine, counts, 0.0), axis=1, keepdims=True)
    place = lax.broadcasted_iota(jnp.int32, (GHOSTS, 1), 0) % CAP
    node = jnp.where(place.astype(jnp.float32) < used, node, -1.0).astype(jnp.int32)
    return jnp.where(lax.broadcasted_iota(jnp.int32, (GHOSTS, NP), 1) == node, 1.0, 0.0).astype(jnp.bfloat16)


def pack(rows, send_ref, count_ref, packed_ref):
    hot = packing_one_hot(send_ref[...], count_ref[...])
    high = rows.astype(jnp.bfloat16)
    low = (rows - high.astype(jnp.float32)).astype(jnp.bfloat16)
    dims = (((1,), (1,)), ((), ()))
    packed_ref[:, :ROWS] = lax.dot_general(hot, high, dims, preferred_element_type=jnp.float32) + lax.dot_general(
        hot, low, dims, preferred_element_type=jnp.float32
    )
    packed_ref[:, ROWS:] = jnp.zeros((GHOSTS, LANES - ROWS), jnp.float32)


def directions():
    place = lax.broadcasted_iota(jnp.int32, (8, 128), 0)
    within = [jnp.full((8, 128), 0.0, jnp.float32)] * 2
    for row in range(8):
        angle = (row + 0.5) * 2.0 * math.pi / ND
        within = [jnp.where(place == row, jnp.float32(g(angle)), old) for g, old in zip((math.cos, math.sin), within)]
    inner_cosine, inner_sine = within
    cosine, sine = [], []
    for tile in range(PAIR // 8):
        angle = 8 * tile * 2.0 * math.pi / ND
        outer_cosine, outer_sine = jnp.float32(math.cos(angle)), jnp.float32(math.sin(angle))
        cosine.append(outer_cosine * inner_cosine - outer_sine * inner_sine)
        sine.append(outer_sine * inner_cosine + outer_cosine * inner_sine)
    return [jnp.concatenate([jnp.concatenate(tiles, axis=0)] * (NP // 128), axis=1) for tiles in (cosine, sine)]


def delta(got, coords, axis):
    row = COORDS + 2 * axis
    return (got[row : row + 1] + got[row + 1 : row + 2]) - coords[axis : axis + 1]


def facing(cosine, sine, delta_x, delta_y):
    return jnp.maximum(-(cosine * delta_x + sine * delta_y), 0.0)


def add_slot(target_ref, source_ref, inflow, got, fresh):
    for start, size in GROUPS:
        rows = slice(start, start + size)
        term = inflow[:size] * got[rows]
        target_ref[rows] = term if fresh else source_ref[rows] + term


def rolled(x, shift):
    shift = shift % ND
    return jnp.concatenate([x[ND - shift :], x[: ND - shift]], axis=0)


def pack_kernel(
    band_ref, spectra_hbm, coords_hbm, send_hbm, count_hbm, wind_hbm, area_hbm, near_hbm,
    packed_ref, spectra_ref, coords_ref, send_ref, count_ref, wind_ref, area_ref, near_ref, near_edge_ref, far_edge_ref,
    rows_ref, sems,
):
    odd = lax.rem(band_ref[0], 2)
    inner = pl.ds((1 - odd) * (BAND - DOWN_REACH), DOWN_REACH)
    outer = pl.ds(odd * (BAND - DOWN_REACH), DOWN_REACH)
    pairs = (
        (spectra_hbm, spectra_ref),
        (coords_hbm, coords_ref),
        (send_hbm, send_ref),
        (count_hbm, count_ref),
        (spectra_hbm.at[inner], near_edge_ref),
        (spectra_hbm.at[outer], far_edge_ref),
        (wind_hbm, wind_ref),
        (area_hbm, area_ref),
        (near_hbm, near_ref),
    )
    copies = [pltpu.make_async_copy(source, target, sems.at[i]) for i, (source, target) in enumerate(pairs)]
    for copy in copies:
        copy.start()
    for copy in copies[:4]:
        copy.wait()
    fill_rows(rows_ref, spectra_ref, coords_ref)
    pack(rows_ref[...], send_ref, count_ref, packed_ref)
    for copy in copies[4:]:
        copy.wait()


def local_kernel(
    band_ref, spectra_ref, near_edge_ref, far_edge_ref, coords_ref, wind_ref, area_ref, near_ref,
    base_ref, partial_ref, rows_ref,
):
    band = band_ref[0]
    coords = coords_ref[...]
    fill_rows(rows_ref, spectra_ref, coords_ref)
    pieces = bf16_pieces(rows_ref[...])
    cosine, sine = directions()
    for k in range(K):
        entry = near_ref[k : k + 1, :]
        got = gather(pieces, entry, 0)
        delta_x = jnp.where(entry < NP, delta(got, coords, 0), 0.0)
        delta_y = jnp.where(entry < NP, delta(got, coords, 1), 0.0)
        partial_ref[ROWS + k : ROWS + k + 1] = delta_x
        partial_ref[ROWS + K + k : ROWS + K + k + 1] = delta_y
        add_slot(partial_ref, partial_ref, facing(cosine, sine, delta_x, delta_y), got, k == 0)
    partial_ref[ROWS + 2 * K : ROWS + 2 * K + 1] = area_ref[...]
    along = cosine[:ND] * wind_ref[0:1, :] + sine[:ND] * wind_ref[1:2, :]
    odd = lax.rem(band, 2) == 1
    lower = [jnp.where(odd, near_edge_ref[f], far_edge_ref[f]) for f in range(DOWN_REACH)]
    upper = [jnp.where(odd, far_edge_ref[f], near_edge_ref[f]) for f in range(UP_REACH)]
    base_ref[COORDS:] = jnp.zeros((ROWS - COORDS, NP), jnp.float32)
    for f in range(BAND):
        density = spectra_ref[f]
        up = spectra_ref[f + UP_REACH] if f + UP_REACH < BAND else upper[f + UP_REACH - BAND]
        down = spectra_ref[f - DOWN_REACH] if f >= DOWN_REACH else lower[f]
        up_left, up_right = rolled(up, -UP_SHIFT), rolled(up, UP_SHIFT)
        down_left, down_right = rolled(down, DOWN_SHIFT), rolled(down, -DOWN_SHIFT)
        quad = quad_coupling * (
            density * density * (up_left + down_left + up_right + down_right)
            - 2.0 * density * (up_left * down_left + up_right * down_right)
        )
        growth = wind_growth * jnp.maximum(ratio_of(band, f) * along - 1.0, 0.0)
        base_ref[f * ND : (f + 1) * ND] = density + time_step * (quad + growth * density)


def settle(band, base_ref, area, total_ref, weight, group, target_ref):
    start, size = group
    rows = slice(start, start + size)
    lower, upper = start // ND, min(start // ND + 1, BAND - 1)
    row = lax.broadcasted_iota(jnp.int32, (size, NP), 0)
    scaled = jnp.where(row < ND, scale_of(band, lower), scale_of(band, upper)) * area
    target_ref[rows] = (base_ref[rows] + scaled * total_ref[rows]) / (1.0 + scaled * weight[:size])


def ghost_pieces(ghost_ref):
    return bf16_pieces(ghost_ref[...].T[:ROWS])


def first_kernel(
    band_ref, ghost_ref, base_ref, partial_ref, coords_ref, near_ref, send_ref, count_ref,
    packed_ref, total_ref, delta_ref,
):
    band = band_ref[0]
    coords = coords_ref[...]
    pieces = ghost_pieces(ghost_ref)
    cosine, sine = directions()
    weight = jnp.zeros((PAIR, NP), jnp.float32)
    for k in range(K):
        entry = near_ref[k : k + 1, :]
        got = gather(pieces, entry, NP)
        delta_x = jnp.where(entry < NP, partial_ref[ROWS + k : ROWS + k + 1], delta(got, coords, 0))
        delta_y = jnp.where(entry < NP, partial_ref[ROWS + K + k : ROWS + K + k + 1], delta(got, coords, 1))
        delta_ref[k : k + 1, :] = delta_x
        delta_ref[K + k : K + k + 1, :] = delta_y
        inflow = facing(cosine, sine, delta_x, delta_y)
        weight = weight + inflow
        add_slot(total_ref, partial_ref if k == 0 else total_ref, inflow, got, False)
    area = partial_ref[ROWS + 2 * K : ROWS + 2 * K + 1]
    delta_ref[2 * K : 2 * K + 1, :] = area
    for group in GROUPS:
        settle(band, base_ref, area, total_ref, weight, group, total_ref)
    pack(total_ref[...], send_ref, count_ref, packed_ref)


def second_local_kernel(current_ref, delta_ref, near_ref, partial_ref):
    pieces = bf16_pieces(current_ref[...])
    cosine, sine = directions()
    for k in range(K):
        got = gather(pieces, near_ref[k : k + 1, :], 0)
        inflow = facing(cosine, sine, delta_ref[k : k + 1, :], delta_ref[K + k : K + k + 1, :])
        add_slot(partial_ref, partial_ref, inflow, got, k == 0)


def second_kernel(
    band_ref, ghost_ref, base_ref, partial_ref, delta_ref, near_ref, out_ref, total_ref, planes_ref, sems
):
    band = band_ref[0]
    pieces = ghost_pieces(ghost_ref)
    cosine, sine = directions()
    weight = jnp.zeros((PAIR, NP), jnp.float32)
    for k in range(K):
        got = gather(pieces, near_ref[k : k + 1, :], NP)
        inflow = facing(cosine, sine, delta_ref[k : k + 1, :], delta_ref[K + k : K + k + 1, :])
        weight = weight + inflow
        add_slot(total_ref, partial_ref if k == 0 else total_ref, inflow, got, False)
    area = delta_ref[2 * K : 2 * K + 1, :]
    copies = []
    for index, group in enumerate(GROUPS):
        settle(band, base_ref, area, total_ref, weight, group, total_ref)
        first = 2 * index
        count = min(2, BAND - first)
        for f in range(first, first + count):
            planes_ref[f] = total_ref[f * ND : (f + 1) * ND]
        moved = pl.ds(first, count)
        copies.append(pltpu.make_async_copy(planes_ref.at[moved], out_ref.at[moved], sems.at[index]))
        copies[-1].start()
    for copy in copies:
        copy.wait()


VMEM, SMEM, HBM = pltpu.VMEM, pltpu.SMEM, pltpu.HBM


def call(kernel, outs, scratch, name, *operands):
    return pl.pallas_call(
        kernel,
        out_shape=[jax.ShapeDtypeStruct(shape, dtype) for shape, dtype, _ in outs],
        in_specs=[pl.BlockSpec(memory_space=memory) for _, memory in operands],
        out_specs=[pl.BlockSpec(memory_space=memory) for _, _, memory in outs],
        scratch_shapes=scratch,
        compiler_params=pltpu.CompilerParams(vmem_limit_bytes=24 << 20),
        name=name,
        cost_estimate=pl.CostEstimate(flops=10**10, transcendentals=0, bytes_accessed=10**10),
    )(*[pltpu.with_memory_space_constraint(array, HBM) if memory is HBM else array for array, memory in operands])


def local(spectra, coords, inv_area, wind_vector, neighbours, send_nodes, send_count):
    bands = lax.axis_size("freq")
    band = lax.axis_index("freq").astype(jnp.int32).reshape(1)
    f32, planes = jnp.float32, (BAND, ND, NP)
    rows, dma = pltpu.VMEM((ROWS, NP), f32), pltpu.SemaphoreType.DMA
    send, count, area = send_nodes.T, send_count.reshape(1, -1), inv_area.reshape(1, -1)

    def exchange(packed):
        packed = packed.reshape(N_MESH, CAP, LANES)
        return lax.all_to_all(packed, "mesh", split_axis=0, concat_axis=0, tiled=True).reshape(GHOSTS, LANES)

    def inside(*arrays):
        return [(array, VMEM) for array in arrays]

    inputs = (spectra, coords, send, count, wind_vector, area, neighbours)
    packed, spectra, coords, send, count, wind, area, near, near_edge, far_edge = call(
        pack_kernel,
        [((GHOSTS, LANES), f32, VMEM)]
        + [(array.shape, array.dtype, VMEM) for array in inputs]
        + [((DOWN_REACH, ND, NP), f32, VMEM)] * 2,
        [rows, dma((len(inputs) + 2,))],
        "pack",
        (band, SMEM),
        *[(array, HBM) for array in inputs],
    )
    pairs = [[pair for i in range(start, bands - 1, 2) for pair in ((i, i + 1), (i + 1, i))] for start in (0, 1)]
    near_edge = lax.ppermute(near_edge, "freq", pairs[0])
    far_edge = lax.ppermute(far_edge, "freq", pairs[1])
    ghosts = exchange(packed)
    base, partial = call(
        local_kernel,
        [((ROWS, NP), f32, VMEM), ((ROWS + 3 * K, NP), f32, VMEM)],
        [rows],
        "local_first",
        (band, SMEM),
        *inside(spectra, near_edge, far_edge, coords, wind, area, near),
    )
    packed, current, deltas = call(
        first_kernel,
        [((GHOSTS, LANES), f32, VMEM), ((ROWS, NP), f32, VMEM), ((3 * K, NP), f32, VMEM)],
        [],
        "first",
        (band, SMEM),
        *inside(ghosts, base, partial, coords, near, send, count),
    )
    ghosts = exchange(packed)
    (partial,) = call(
        second_local_kernel, [((ROWS, NP), f32, VMEM)], [], "local_second", *inside(current, deltas, near)
    )
    (updated,) = call(
        second_kernel,
        [(planes, f32, HBM)],
        [rows, pltpu.VMEM(planes, f32), dma((len(GROUPS),))],
        "second",
        (band, SMEM),
        *inside(ghosts, base, partial, deltas, near),
    )
    return updated


def solution(mesh):
    in_specs = (
        P("freq", None, "mesh"),
        P(None, "mesh"),
        P("mesh"),
        P(None, "mesh"),
        P(None, "mesh"),
        P("mesh", None),
        P("mesh"),
    )
    out_specs = P("freq", None, "mesh")
    return jax.shard_map(local, mesh=mesh, in_specs=in_specs, out_specs=out_specs, check_vma=False)
```

```python
import math

import jax
import jax.numpy as jnp
import numpy as np
from jax import lax
from jax.experimental import pallas as pl
from jax.experimental.pallas import tpu as pltpu
from jax.sharding import PartitionSpec as P

NF = 36
ND = 36
K = 8
NP = 512
CAP = 8
N_MESH = 32
GHOSTS = N_MESH * CAP
BAND = 9
UP_REACH = 2
DOWN_REACH = 3
UP_SHIFT = 1
DOWN_SHIFT = 3
COORDS = BAND * ND
ROWS = COORDS + 4
LANES = 384
PAIR = 2 * ND
GROUPS = [(0, PAIR), (PAIR, PAIR), (2 * PAIR, PAIR), (3 * PAIR, PAIR), (4 * PAIR, ROWS - 4 * PAIR)]

time_step = 0.5
group_scale = 0.8
quad_coupling = 0.25
wind_growth = 0.1
RATIOS = np.power(np.float64(1.1), np.arange(NF) - NF // 2)


def rounded(x):
    return x.astype(jnp.bfloat16).astype(jnp.float32)


def bf16_pieces(x):
    high = rounded(x)
    return jnp.concatenate([high, x - high], axis=0).astype(jnp.bfloat16)


def pieces_with_coords(x):
    top = []
    for axis in range(2):
        row = COORDS + 2 * axis
        high = rounded(x[row : row + 1])
        top += [high, x[row : row + 1] - high, x[row + 1 : row + 2]]
    top.append(jnp.zeros((2, x.shape[1]), jnp.float32))
    high = rounded(x)
    return jnp.concatenate([jnp.concatenate(top, axis=0), high, x - high], axis=0).astype(jnp.bfloat16)


def exact_rows(c):
    high = rounded(c)
    mid = rounded(c - high)
    return high + mid, (c - high) - mid


def by_band(band, values):
    picked = jnp.float32(values[3])
    for index in (2, 1, 0):
        picked = jnp.where(band == index, jnp.float32(values[index]), picked)
    return picked


def ratio_of(band, f):
    return by_band(band, [RATIOS[b * BAND + f] for b in range(NF // BAND)])


def scale_of(band, f):
    return by_band(band, [time_step * group_scale / RATIOS[b * BAND + f] for b in range(NF // BAND)])


def one_hot(entry_row, first, count):
    node = lax.broadcasted_iota(jnp.int32, (count, entry_row.shape[1]), 0) + first
    return jnp.where(node == entry_row, 1.0, 0.0).astype(jnp.bfloat16)


def gather(pieces, entry_row, first):
    got = jnp.dot(pieces, one_hot(entry_row, first, pieces.shape[1]), preferred_element_type=jnp.float32)
    top = got.shape[0] - 2 * ROWS
    return got[:top], got[top : top + ROWS] + got[top + ROWS :]


def fill_coords(rows_ref, coords_ref):
    for axis in range(2):
        first, second = exact_rows(coords_ref[axis : axis + 1, :])
        rows_ref[COORDS + 2 * axis : COORDS + 2 * axis + 1, :] = first
        rows_ref[COORDS + 2 * axis + 1 : COORDS + 2 * axis + 2, :] = second


def fill_rows(rows_ref, spectra_ref, coords_ref):
    for f in range(BAND):
        rows_ref[f * ND : (f + 1) * ND, :] = spectra_ref[f]
    fill_coords(rows_ref, coords_ref)


def packing_one_hot(send, count):
    slots = jnp.concatenate([send.astype(jnp.float32)] * N_MESH, axis=0)
    counts = jnp.broadcast_to(count.astype(jnp.float32), slots.shape)
    row = lax.broadcasted_iota(jnp.int32, slots.shape, 0)
    mine = lax.broadcasted_iota(jnp.int32, slots.shape, 1) == row // CAP
    node = jnp.sum(jnp.where(mine, slots, 0.0), axis=1, keepdims=True)
    used = jnp.sum(jnp.where(mine, counts, 0.0), axis=1, keepdims=True)
    place = lax.broadcasted_iota(jnp.int32, (GHOSTS, 1), 0) % CAP
    node = jnp.where(place.astype(jnp.float32) < used, node, -1.0).astype(jnp.int32)
    return jnp.where(lax.broadcasted_iota(jnp.int32, (GHOSTS, NP), 1) == node, 1.0, 0.0).astype(jnp.bfloat16)


def pack(hot, rows, packed_ref):
    high = rows.astype(jnp.bfloat16)
    low = (rows - high.astype(jnp.float32)).astype(jnp.bfloat16)
    dims = (((1,), (1,)), ((), ()))
    packed_ref[:, :ROWS] = lax.dot_general(hot, high, dims, preferred_element_type=jnp.float32) + lax.dot_general(
        hot, low, dims, preferred_element_type=jnp.float32
    )
    packed_ref[:, ROWS:] = jnp.zeros((GHOSTS, LANES - ROWS), jnp.float32)


def directions():
    place = lax.broadcasted_iota(jnp.int32, (8, 128), 0)
    within = [jnp.full((8, 128), 0.0, jnp.float32)] * 2
    for row in range(8):
        angle = (row + 0.5) * 2.0 * math.pi / ND
        within = [jnp.where(place == row, jnp.float32(g(angle)), old) for g, old in zip((math.cos, math.sin), within)]
    inner_cosine, inner_sine = within
    cosine, sine = [], []
    for tile in range(PAIR // 8):
        angle = 8 * tile * 2.0 * math.pi / ND
        outer_cosine, outer_sine = jnp.float32(math.cos(angle)), jnp.float32(math.sin(angle))
        cosine.append(outer_cosine * inner_cosine - outer_sine * inner_sine)
        sine.append(outer_sine * inner_cosine + outer_cosine * inner_sine)
    return [jnp.concatenate([jnp.concatenate(tiles, axis=0)] * (NP // 128), axis=1) for tiles in (cosine, sine)]


def delta(place, coords, axis):
    row = 3 * axis
    return ((place[row : row + 1] + place[row + 1 : row + 2]) + place[row + 2 : row + 3]) - coords[axis : axis + 1]


def facing(cosine, sine, delta_x, delta_y):
    return jnp.maximum(-(cosine * delta_x + sine * delta_y), 0.0)


def add_slot(target_ref, source_ref, inflow, got, fresh):
    for start, size in GROUPS:
        rows = slice(start, start + size)
        term = inflow[:size] * got[rows]
        target_ref[rows] = term if fresh else source_ref[rows] + term


def rolled(x, shift):
    shift = shift % ND
    return jnp.concatenate([x[ND - shift :], x[: ND - shift]], axis=0)


def pack_kernel(
    band_ref, spectra_hbm, coords_hbm, send_hbm, count_hbm, wind_hbm, area_hbm, near_hbm,
    packed_ref, spectra_ref, coords_ref, send_ref, count_ref, wind_ref, area_ref, near_ref, near_edge_ref, far_edge_ref,
    rows_ref, hot_ref, sems,
):
    odd = lax.rem(band_ref[0], 2)
    inner = pl.ds((1 - odd) * (BAND - DOWN_REACH), DOWN_REACH)
    outer = pl.ds(odd * (BAND - DOWN_REACH), DOWN_REACH)
    pairs = (
        (send_hbm, send_ref),
        (count_hbm, count_ref),
        (spectra_hbm, spectra_ref),
        (coords_hbm, coords_ref),
        (spectra_hbm.at[inner], near_edge_ref),
        (spectra_hbm.at[outer], far_edge_ref),
        (wind_hbm, wind_ref),
        (area_hbm, area_ref),
        (near_hbm, near_ref),
    )
    copies = [pltpu.make_async_copy(source, target, sems.at[i]) for i, (source, target) in enumerate(pairs)]
    for copy in copies:
        copy.start()
    for copy in copies[:2]:
        copy.wait()
    hot_ref[...] = packing_one_hot(send_ref[...], count_ref[...])
    for copy in copies[2:4]:
        copy.wait()
    fill_rows(rows_ref, spectra_ref, coords_ref)
    pack(hot_ref[...], rows_ref[...], packed_ref)
    for copy in copies[4:]:
        copy.wait()


def local_kernel(spectra_ref, coords_ref, area_ref, near_ref, partial_ref, rows_ref):
    coords = coords_ref[...]
    fill_rows(rows_ref, spectra_ref, coords_ref)
    pieces = pieces_with_coords(rows_ref[...])
    cosine, sine = directions()
    for k in range(K):
        entry = near_ref[k : k + 1, :]
        place, got = gather(pieces, entry, 0)
        delta_x = jnp.where(entry < NP, delta(place, coords, 0), 0.0)
        delta_y = jnp.where(entry < NP, delta(place, coords, 1), 0.0)
        partial_ref[ROWS + k : ROWS + k + 1] = delta_x
        partial_ref[ROWS + K + k : ROWS + K + k + 1] = delta_y
        add_slot(partial_ref, partial_ref, facing(cosine, sine, delta_x, delta_y), got, k == 0)
    partial_ref[ROWS + 2 * K : ROWS + 2 * K + 1] = area_ref[...]


def source_kernel(band_ref, spectra_ref, near_edge_ref, far_edge_ref, wind_ref, base_ref):
    band = band_ref[0]
    cosine, sine = directions()
    along = cosine[:ND] * wind_ref[0:1, :] + sine[:ND] * wind_ref[1:2, :]
    odd = lax.rem(band, 2) == 1
    lower = [jnp.where(odd, near_edge_ref[f], far_edge_ref[f]) for f in range(DOWN_REACH)]
    upper = [jnp.where(odd, far_edge_ref[f], near_edge_ref[f]) for f in range(UP_REACH)]
    base_ref[COORDS:] = jnp.zeros((ROWS - COORDS, NP), jnp.float32)

    def source(f):
        density = spectra_ref[f]
        up = spectra_ref[f + UP_REACH] if f + UP_REACH < BAND else upper[f + UP_REACH - BAND]
        down = spectra_ref[f - DOWN_REACH] if f >= DOWN_REACH else lower[f]
        up_left, up_right = rolled(up, -UP_SHIFT), rolled(up, UP_SHIFT)
        down_left, down_right = rolled(down, DOWN_SHIFT), rolled(down, -DOWN_SHIFT)
        quad = quad_coupling * (
            density * density * (up_left + down_left + up_right + down_right)
            - 2.0 * density * (up_left * down_left + up_right * down_right)
        )
        growth = wind_growth * jnp.maximum(ratio_of(band, f) * along - 1.0, 0.0)
        base_ref[f * ND : (f + 1) * ND] = density + time_step * (quad + growth * density)

    for f in range(BAND):
        source(f)


def settle(band, base_ref, area, total_ref, weight, group, target_ref):
    start, size = group
    rows = slice(start, start + size)
    lower, upper = start // ND, min(start // ND + 1, BAND - 1)
    row = lax.broadcasted_iota(jnp.int32, (size, NP), 0)
    scaled = jnp.where(row < ND, scale_of(band, lower), scale_of(band, upper)) * area
    target_ref[rows] = (base_ref[rows] + scaled * total_ref[rows]) / (1.0 + scaled * weight[:size])


def ghost_rows(ghost_ref):
    return ghost_ref[...].T[:ROWS]


def first_kernel(
    band_ref, ghost_ref, base_ref, partial_ref, coords_ref, near_ref, send_ref, count_ref,
    packed_ref, total_ref, delta_ref,
):
    band = band_ref[0]
    coords = coords_ref[...]
    pieces = pieces_with_coords(ghost_rows(ghost_ref))
    cosine, sine = directions()
    weight = jnp.zeros((PAIR, NP), jnp.float32)
    for k in range(K):
        entry = near_ref[k : k + 1, :]
        place, got = gather(pieces, entry, NP)
        delta_x = jnp.where(entry < NP, partial_ref[ROWS + k : ROWS + k + 1], delta(place, coords, 0))
        delta_y = jnp.where(entry < NP, partial_ref[ROWS + K + k : ROWS + K + k + 1], delta(place, coords, 1))
        delta_ref[k : k + 1, :] = delta_x
        delta_ref[K + k : K + k + 1, :] = delta_y
        inflow = facing(cosine, sine, delta_x, delta_y)
        weight = weight + inflow
        add_slot(total_ref, partial_ref if k == 0 else total_ref, inflow, got, False)
    area = partial_ref[ROWS + 2 * K : ROWS + 2 * K + 1]
    delta_ref[2 * K : 2 * K + 1, :] = area
    for group in GROUPS:
        settle(band, base_ref, area, total_ref, weight, group, total_ref)
    pack(packing_one_hot(send_ref[...], count_ref[...]), total_ref[...], packed_ref)


def second_local_kernel(current_ref, delta_ref, near_ref, partial_ref):
    pieces = bf16_pieces(current_ref[...])
    cosine, sine = directions()
    for k in range(K):
        _, got = gather(pieces, near_ref[k : k + 1, :], 0)
        inflow = facing(cosine, sine, delta_ref[k : k + 1, :], delta_ref[K + k : K + k + 1, :])
        add_slot(partial_ref, partial_ref, inflow, got, k == 0)


def second_kernel(
    band_ref, ghost_ref, base_ref, partial_ref, delta_ref, near_ref, out_ref, total_ref, planes_ref, sems
):
    band = band_ref[0]
    pieces = bf16_pieces(ghost_rows(ghost_ref))
    cosine, sine = directions()
    weight = jnp.zeros((PAIR, NP), jnp.float32)
    for k in range(K):
        _, got = gather(pieces, near_ref[k : k + 1, :], NP)
        inflow = facing(cosine, sine, delta_ref[k : k + 1, :], delta_ref[K + k : K + k + 1, :])
        weight = weight + inflow
        add_slot(total_ref, partial_ref if k == 0 else total_ref, inflow, got, False)
    area = delta_ref[2 * K : 2 * K + 1, :]
    copies = []
    for index, group in enumerate(GROUPS):
        settle(band, base_ref, area, total_ref, weight, group, total_ref)
        first = 2 * index
        count = min(2, BAND - first)
        for f in range(first, first + count):
            planes_ref[f] = total_ref[f * ND : (f + 1) * ND]
        moved = pl.ds(first, count)
        copies.append(pltpu.make_async_copy(planes_ref.at[moved], out_ref.at[moved], sems.at[index]))
        copies[-1].start()
    for copy in copies:
        copy.wait()


VMEM, SMEM, HBM = pltpu.VMEM, pltpu.SMEM, pltpu.HBM


def call(kernel, outs, scratch, name, *operands):
    return pl.pallas_call(
        kernel,
        out_shape=[jax.ShapeDtypeStruct(shape, dtype) for shape, dtype, _ in outs],
        in_specs=[pl.BlockSpec(memory_space=memory) for _, memory in operands],
        out_specs=[pl.BlockSpec(memory_space=memory) for _, _, memory in outs],
        scratch_shapes=scratch,
        compiler_params=pltpu.CompilerParams(vmem_limit_bytes=24 << 20),
        name=name,
    )(*[pltpu.with_memory_space_constraint(array, HBM) if memory is HBM else array for array, memory in operands])


def local(spectra, coords, inv_area, wind_vector, neighbours, send_nodes, send_count):
    bands = lax.axis_size("freq")
    band = lax.axis_index("freq").astype(jnp.int32).reshape(1)
    f32, planes = jnp.float32, (BAND, ND, NP)
    rows, dma = pltpu.VMEM((ROWS, NP), f32), pltpu.SemaphoreType.DMA
    send, count, area = send_nodes.T, send_count.reshape(1, -1), inv_area.reshape(1, -1)

    def exchange(packed):
        packed = packed.reshape(N_MESH, CAP, LANES)
        return lax.all_to_all(packed, "mesh", split_axis=0, concat_axis=0, tiled=True).reshape(GHOSTS, LANES)

    def inside(*arrays):
        return [(array, VMEM) for array in arrays]

    inputs = (spectra, coords, send, count, wind_vector, area, neighbours)
    packed, spectra, coords, send, count, wind, area, near, near_edge, far_edge = call(
        pack_kernel,
        [((GHOSTS, LANES), f32, VMEM)]
        + [(array.shape, array.dtype, VMEM) for array in inputs]
        + [((DOWN_REACH, ND, NP), f32, VMEM)] * 2,
        [rows, pltpu.VMEM((GHOSTS, NP), jnp.bfloat16), dma((len(inputs) + 2,))],
        "pack",
        (band, SMEM),
        *[(array, HBM) for array in inputs],
    )
    pairs = [[pair for i in range(start, bands - 1, 2) for pair in ((i, i + 1), (i + 1, i))] for start in (0, 1)]
    near_edge = lax.ppermute(near_edge, "freq", pairs[0])
    far_edge = lax.ppermute(far_edge, "freq", pairs[1])
    ghosts = exchange(packed)
    (partial,) = call(
        local_kernel,
        [((ROWS + 3 * K, NP), f32, VMEM)],
        [rows],
        "local_first",
        *inside(spectra, coords, area, near),
    )
    (base,) = call(
        source_kernel,
        [((ROWS, NP), f32, VMEM)],
        [],
        "source",
        (band, SMEM),
        *inside(spectra, near_edge, far_edge, wind),
    )
    packed, current, deltas = call(
        first_kernel,
        [((GHOSTS, LANES), f32, VMEM), ((ROWS, NP), f32, VMEM), ((3 * K, NP), f32, VMEM)],
        [],
        "first",
        (band, SMEM),
        *inside(ghosts, base, partial, coords, near, send, count),
    )
    ghosts = exchange(packed)
    (partial,) = call(
        second_local_kernel, [((ROWS, NP), f32, VMEM)], [], "local_second", *inside(current, deltas, near)
    )
    (updated,) = call(
        second_kernel,
        [(planes, f32, HBM)],
        [rows, pltpu.VMEM(planes, f32), dma((len(GROUPS),))],
        "second",
        (band, SMEM),
        *inside(ghosts, base, partial, deltas, near),
    )
    return updated


def solution(mesh):
    in_specs = (
        P("freq", None, "mesh"),
        P(None, "mesh"),
        P("mesh"),
        P(None, "mesh"),
        P(None, "mesh"),
        P("mesh", None),
        P("mesh"),
    )
    out_specs = P("freq", None, "mesh")
    return jax.shard_map(local, mesh=mesh, in_specs=in_specs, out_specs=out_specs, check_vma=False)
```

```python
import math

import jax
import jax.numpy as jnp
import numpy as np
from jax import lax
from jax.experimental import pallas as pl
from jax.experimental.pallas import tpu as pltpu
from jax.sharding import PartitionSpec as P

NF = 36
ND = 36
K = 8
NP = 512
CAP = 8
N_MESH = 32
GHOSTS = N_MESH * CAP
BAND = 9
UP_REACH = 2
DOWN_REACH = 3
UP_SHIFT = 1
DOWN_SHIFT = 3
COORDS = BAND * ND
ROWS = COORDS + 4
LANES = 384
PAIR = 2 * ND
GROUPS = [(0, PAIR), (PAIR, PAIR), (2 * PAIR, PAIR), (3 * PAIR, PAIR), (4 * PAIR, ROWS - 4 * PAIR)]

time_step = 0.5
group_scale = 0.8
quad_coupling = 0.25
wind_growth = 0.1
RATIOS = np.power(np.float64(1.1), np.arange(NF) - NF // 2)


def rounded(x):
    return x.astype(jnp.bfloat16).astype(jnp.float32)


def bf16_pieces(x):
    high = rounded(x)
    return jnp.concatenate([high, x - high], axis=0).astype(jnp.bfloat16)


def pieces_with_coords(x):
    top = []
    for axis in range(2):
        row = COORDS + 2 * axis
        high = rounded(x[row : row + 1])
        top += [high, x[row : row + 1] - high, x[row + 1 : row + 2]]
    top.append(jnp.zeros((2, x.shape[1]), jnp.float32))
    high = rounded(x)
    return jnp.concatenate([jnp.concatenate(top, axis=0), high, x - high], axis=0).astype(jnp.bfloat16)


def exact_rows(c):
    high = rounded(c)
    mid = rounded(c - high)
    return high + mid, (c - high) - mid


def by_band(band, values):
    picked = jnp.float32(values[3])
    for index in (2, 1, 0):
        picked = jnp.where(band == index, jnp.float32(values[index]), picked)
    return picked


def ratio_of(band, f):
    return by_band(band, [RATIOS[b * BAND + f] for b in range(NF // BAND)])


def scale_of(band, f):
    return by_band(band, [time_step * group_scale / RATIOS[b * BAND + f] for b in range(NF // BAND)])


def one_hot(entry_row, first, count):
    node = lax.broadcasted_iota(jnp.int32, (count, entry_row.shape[1]), 0) + first
    return jnp.where(node == entry_row, 1.0, 0.0).astype(jnp.bfloat16)


def gather(pieces, entry_row, first):
    got = jnp.dot(pieces, one_hot(entry_row, first, pieces.shape[1]), preferred_element_type=jnp.float32)
    top = got.shape[0] - 2 * ROWS
    return got[:top], got[top : top + ROWS] + got[top + ROWS :]


def fill_coords(rows_ref, coords_ref):
    for axis in range(2):
        first, second = exact_rows(coords_ref[axis : axis + 1, :])
        rows_ref[COORDS + 2 * axis : COORDS + 2 * axis + 1, :] = first
        rows_ref[COORDS + 2 * axis + 1 : COORDS + 2 * axis + 2, :] = second


def fill_rows(rows_ref, spectra_ref, coords_ref):
    for f in range(BAND):
        rows_ref[f * ND : (f + 1) * ND, :] = spectra_ref[f]
    fill_coords(rows_ref, coords_ref)


def packing_one_hot(send, count):
    slots = jnp.concatenate([send.astype(jnp.float32)] * N_MESH, axis=0)
    counts = jnp.broadcast_to(count.astype(jnp.float32), slots.shape)
    row = lax.broadcasted_iota(jnp.int32, slots.shape, 0)
    mine = lax.broadcasted_iota(jnp.int32, slots.shape, 1) == row // CAP
    node = jnp.sum(jnp.where(mine, slots, 0.0), axis=1, keepdims=True)
    used = jnp.sum(jnp.where(mine, counts, 0.0), axis=1, keepdims=True)
    place = lax.broadcasted_iota(jnp.int32, (GHOSTS, 1), 0) % CAP
    node = jnp.where(place.astype(jnp.float32) < used, node, -1.0).astype(jnp.int32)
    return jnp.where(lax.broadcasted_iota(jnp.int32, (GHOSTS, NP), 1) == node, 1.0, 0.0).astype(jnp.bfloat16)


def pack(hot, rows, packed_ref):
    high = rows.astype(jnp.bfloat16)
    low = (rows - high.astype(jnp.float32)).astype(jnp.bfloat16)
    dims = (((1,), (1,)), ((), ()))
    packed_ref[:, :ROWS] = lax.dot_general(hot, high, dims, preferred_element_type=jnp.float32) + lax.dot_general(
        hot, low, dims, preferred_element_type=jnp.float32
    )
    packed_ref[:, ROWS:] = jnp.zeros((GHOSTS, LANES - ROWS), jnp.float32)


def directions():
    place = lax.broadcasted_iota(jnp.int32, (8, 128), 0)
    within = [jnp.full((8, 128), 0.0, jnp.float32)] * 2
    for row in range(8):
        angle = (row + 0.5) * 2.0 * math.pi / ND
        within = [jnp.where(place == row, jnp.float32(g(angle)), old) for g, old in zip((math.cos, math.sin), within)]
    inner_cosine, inner_sine = within
    cosine, sine = [], []
    for tile in range(PAIR // 8):
        angle = 8 * tile * 2.0 * math.pi / ND
        outer_cosine, outer_sine = jnp.float32(math.cos(angle)), jnp.float32(math.sin(angle))
        cosine.append(outer_cosine * inner_cosine - outer_sine * inner_sine)
        sine.append(outer_sine * inner_cosine + outer_cosine * inner_sine)
    return [jnp.concatenate([jnp.concatenate(tiles, axis=0)] * (NP // 128), axis=1) for tiles in (cosine, sine)]


def delta(place, coords, axis):
    row = 3 * axis
    return ((place[row : row + 1] + place[row + 1 : row + 2]) + place[row + 2 : row + 3]) - coords[axis : axis + 1]


def facing(cosine, sine, delta_x, delta_y):
    return jnp.maximum(-(cosine * delta_x + sine * delta_y), 0.0)


def add_slot(target_ref, source_ref, inflow, got, fresh):
    for start, size in GROUPS:
        rows = slice(start, start + size)
        term = inflow[:size] * got[rows]
        target_ref[rows] = term if fresh else source_ref[rows] + term


def rolled(x, shift):
    shift = shift % ND
    return jnp.concatenate([x[ND - shift :], x[: ND - shift]], axis=0)


def pack_kernel(
    band_ref, spectra_hbm, coords_hbm, send_hbm, count_hbm, wind_hbm, area_hbm, near_hbm,
    packed_ref, spectra_ref, coords_ref, send_ref, count_ref, wind_ref, area_ref, near_ref, near_edge_ref, far_edge_ref,
    rows_ref, hot_ref, sems,
):
    odd = lax.rem(band_ref[0], 2)
    inner = pl.ds((1 - odd) * (BAND - DOWN_REACH), DOWN_REACH)
    outer = pl.ds(odd * (BAND - DOWN_REACH), DOWN_REACH)
    pairs = (
        (send_hbm, send_ref),
        (count_hbm, count_ref),
        (spectra_hbm, spectra_ref),
        (coords_hbm, coords_ref),
        (spectra_hbm.at[inner], near_edge_ref),
        (spectra_hbm.at[outer], far_edge_ref),
        (wind_hbm, wind_ref),
        (area_hbm, area_ref),
        (near_hbm, near_ref),
    )
    copies = [pltpu.make_async_copy(source, target, sems.at[i]) for i, (source, target) in enumerate(pairs)]
    for copy in copies:
        copy.start()
    for copy in copies[:2]:
        copy.wait()
    hot_ref[...] = packing_one_hot(send_ref[...], count_ref[...])
    for copy in copies[2:4]:
        copy.wait()
    fill_rows(rows_ref, spectra_ref, coords_ref)
    pack(hot_ref[...], rows_ref[...], packed_ref)
    for copy in copies[4:]:
        copy.wait()


def source(f, band, spectra_ref, lower_ref, upper_ref, along, base_ref):
    density = spectra_ref[f]
    up = spectra_ref[f + UP_REACH] if f + UP_REACH < BAND else upper_ref[f + UP_REACH - BAND]
    down = spectra_ref[f - DOWN_REACH] if f >= DOWN_REACH else lower_ref[f]
    up_left, up_right = rolled(up, -UP_SHIFT), rolled(up, UP_SHIFT)
    down_left, down_right = rolled(down, DOWN_SHIFT), rolled(down, -DOWN_SHIFT)
    quad = quad_coupling * (
        density * density * (up_left + down_left + up_right + down_right)
        - 2.0 * density * (up_left * down_left + up_right * down_right)
    )
    growth = wind_growth * jnp.maximum(ratio_of(band, f) * along - 1.0, 0.0)
    base_ref[f * ND : (f + 1) * ND] = density + time_step * (quad + growth * density)


def edge_sources(is_lower, edge_ref, band, spectra_ref, along, base_ref):
    @pl.when(is_lower)
    def _():
        for f in range(DOWN_REACH):
            source(f, band, spectra_ref, edge_ref, None, along, base_ref)

    @pl.when(jnp.logical_not(is_lower))
    def _():
        for f in range(BAND - UP_REACH, BAND):
            source(f, band, spectra_ref, None, edge_ref, along, base_ref)


def local_kernel(
    band_ref, spectra_ref, near_edge_ref, coords_ref, wind_ref, area_ref, near_ref, base_ref, partial_ref, rows_ref
):
    band = band_ref[0]
    coords = coords_ref[...]
    fill_rows(rows_ref, spectra_ref, coords_ref)
    pieces = pieces_with_coords(rows_ref[...])
    cosine, sine = directions()
    along = cosine[:ND] * wind_ref[0:1, :] + sine[:ND] * wind_ref[1:2, :]
    base_ref[COORDS:] = jnp.zeros((ROWS - COORDS, NP), jnp.float32)
    for f in range(DOWN_REACH, BAND - UP_REACH):
        source(f, band, spectra_ref, None, None, along, base_ref)
    for k in range(K):
        entry = near_ref[k : k + 1, :]
        place, got = gather(pieces, entry, 0)
        delta_x = jnp.where(entry < NP, delta(place, coords, 0), 0.0)
        delta_y = jnp.where(entry < NP, delta(place, coords, 1), 0.0)
        partial_ref[ROWS + k : ROWS + k + 1] = delta_x
        partial_ref[ROWS + K + k : ROWS + K + k + 1] = delta_y
        add_slot(partial_ref, partial_ref, facing(cosine, sine, delta_x, delta_y), got, k == 0)
    partial_ref[ROWS + 2 * K : ROWS + 2 * K + 1] = area_ref[...]
    edge_sources(lax.rem(band, 2) == 1, near_edge_ref, band, spectra_ref, along, base_ref)


def settle(band, base_ref, area, total_ref, weight, group, target_ref):
    start, size = group
    rows = slice(start, start + size)
    lower, upper = start // ND, min(start // ND + 1, BAND - 1)
    row = lax.broadcasted_iota(jnp.int32, (size, NP), 0)
    scaled = jnp.where(row < ND, scale_of(band, lower), scale_of(band, upper)) * area
    target_ref[rows] = (base_ref[rows] + scaled * total_ref[rows]) / (1.0 + scaled * weight[:size])


def ghost_rows(ghost_ref):
    return ghost_ref[...].T[:ROWS]


def first_gather_kernel(ghost_ref, partial_ref, coords_ref, near_ref, total_ref, weight_ref, delta_ref):
    coords = coords_ref[...]
    pieces = pieces_with_coords(ghost_rows(ghost_ref))
    cosine, sine = directions()
    weight = jnp.zeros((PAIR, NP), jnp.float32)
    for k in range(K):
        entry = near_ref[k : k + 1, :]
        place, got = gather(pieces, entry, NP)
        delta_x = jnp.where(entry < NP, partial_ref[ROWS + k : ROWS + k + 1], delta(place, coords, 0))
        delta_y = jnp.where(entry < NP, partial_ref[ROWS + K + k : ROWS + K + k + 1], delta(place, coords, 1))
        delta_ref[k : k + 1, :] = delta_x
        delta_ref[K + k : K + k + 1, :] = delta_y
        inflow = facing(cosine, sine, delta_x, delta_y)
        weight = weight + inflow
        add_slot(total_ref, partial_ref if k == 0 else total_ref, inflow, got, False)
    weight_ref[...] = weight
    delta_ref[2 * K : 2 * K + 1, :] = partial_ref[ROWS + 2 * K : ROWS + 2 * K + 1]


def first_settle_kernel(
    band_ref, spectra_ref, far_edge_ref, wind_ref, part_ref, total_ref, weight_ref, delta_ref, send_ref, count_ref,
    packed_ref, current_ref, base_ref,
):
    band = band_ref[0]
    cosine, sine = directions()
    along = cosine[:ND] * wind_ref[0:1, :] + sine[:ND] * wind_ref[1:2, :]
    base_ref[...] = part_ref[...]
    edge_sources(lax.rem(band, 2) == 0, far_edge_ref, band, spectra_ref, along, base_ref)
    area, weight = delta_ref[2 * K : 2 * K + 1], weight_ref[...]
    for group in GROUPS:
        settle(band, base_ref, area, total_ref, weight, group, current_ref)
    pack(packing_one_hot(send_ref[...], count_ref[...]), current_ref[...], packed_ref)


def second_local_kernel(current_ref, delta_ref, near_ref, partial_ref):
    pieces = bf16_pieces(current_ref[...])
    cosine, sine = directions()
    for k in range(K):
        _, got = gather(pieces, near_ref[k : k + 1, :], 0)
        inflow = facing(cosine, sine, delta_ref[k : k + 1, :], delta_ref[K + k : K + k + 1, :])
        add_slot(partial_ref, partial_ref, inflow, got, k == 0)


def second_kernel(
    band_ref, ghost_ref, base_ref, partial_ref, delta_ref, near_ref, out_ref, total_ref, planes_ref, sems
):
    band = band_ref[0]
    pieces = bf16_pieces(ghost_rows(ghost_ref))
    cosine, sine = directions()
    weight = jnp.zeros((PAIR, NP), jnp.float32)
    for k in range(K):
        _, got = gather(pieces, near_ref[k : k + 1, :], NP)
        inflow = facing(cosine, sine, delta_ref[k : k + 1, :], delta_ref[K + k : K + k + 1, :])
        weight = weight + inflow
        add_slot(total_ref, partial_ref if k == 0 else total_ref, inflow, got, False)
    area = delta_ref[2 * K : 2 * K + 1, :]
    copies = []
    for index, group in enumerate(GROUPS):
        settle(band, base_ref, area, total_ref, weight, group, total_ref)
        first = 2 * index
        count = min(2, BAND - first)
        for f in range(first, first + count):
            planes_ref[f] = total_ref[f * ND : (f + 1) * ND]
        moved = pl.ds(first, count)
        copies.append(pltpu.make_async_copy(planes_ref.at[moved], out_ref.at[moved], sems.at[index]))
        copies[-1].start()
    for copy in copies:
        copy.wait()


VMEM, SMEM, HBM = pltpu.VMEM, pltpu.SMEM, pltpu.HBM


def call(kernel, outs, scratch, name, *operands):
    return pl.pallas_call(
        kernel,
        out_shape=[jax.ShapeDtypeStruct(shape, dtype) for shape, dtype, _ in outs],
        in_specs=[pl.BlockSpec(memory_space=memory) for _, memory in operands],
        out_specs=[pl.BlockSpec(memory_space=memory) for _, _, memory in outs],
        scratch_shapes=scratch,
        compiler_params=pltpu.CompilerParams(vmem_limit_bytes=24 << 20),
        name=name,
    )(*[pltpu.with_memory_space_constraint(array, HBM) if memory is HBM else array for array, memory in operands])


def local(spectra, coords, inv_area, wind_vector, neighbours, send_nodes, send_count):
    bands = lax.axis_size("freq")
    band = lax.axis_index("freq").astype(jnp.int32).reshape(1)
    f32, planes = jnp.float32, (BAND, ND, NP)
    rows, dma = pltpu.VMEM((ROWS, NP), f32), pltpu.SemaphoreType.DMA
    send, count, area = send_nodes.T, send_count.reshape(1, -1), inv_area.reshape(1, -1)

    def exchange(packed):
        packed = packed.reshape(N_MESH, CAP, LANES)
        return lax.all_to_all(packed, "mesh", split_axis=0, concat_axis=0, tiled=True).reshape(GHOSTS, LANES)

    def inside(*arrays):
        return [(array, VMEM) for array in arrays]

    inputs = (spectra, coords, send, count, wind_vector, area, neighbours)
    packed, spectra, coords, send, count, wind, area, near, near_edge, far_edge = call(
        pack_kernel,
        [((GHOSTS, LANES), f32, VMEM)]
        + [(array.shape, array.dtype, VMEM) for array in inputs]
        + [((DOWN_REACH, ND, NP), f32, VMEM)] * 2,
        [rows, pltpu.VMEM((GHOSTS, NP), jnp.bfloat16), dma((len(inputs) + 2,))],
        "pack",
        (band, SMEM),
        *[(array, HBM) for array in inputs],
    )
    pairs = [[pair for i in range(start, bands - 1, 2) for pair in ((i, i + 1), (i + 1, i))] for start in (0, 1)]
    near_edge = lax.ppermute(near_edge, "freq", pairs[0])
    far_edge = lax.ppermute(far_edge, "freq", pairs[1])
    ghosts = exchange(packed)
    base, partial = call(
        local_kernel,
        [((ROWS, NP), f32, VMEM), ((ROWS + 3 * K, NP), f32, VMEM)],
        [rows],
        "local_first",
        (band, SMEM),
        *inside(spectra, near_edge, coords, wind, area, near),
    )
    total, weight, deltas = call(
        first_gather_kernel,
        [((ROWS, NP), f32, VMEM), ((PAIR, NP), f32, VMEM), ((3 * K, NP), f32, VMEM)],
        [],
        "first_gather",
        *inside(ghosts, partial, coords, near),
    )
    packed, current, base = call(
        first_settle_kernel,
        [((GHOSTS, LANES), f32, VMEM), ((ROWS, NP), f32, VMEM), ((ROWS, NP), f32, VMEM)],
        [],
        "first_settle",
        (band, SMEM),
        *inside(spectra, far_edge, wind, base, total, weight, deltas, send, count),
    )
    ghosts = exchange(packed)
    (partial,) = call(
        second_local_kernel, [((ROWS, NP), f32, VMEM)], [], "local_second", *inside(current, deltas, near)
    )
    (updated,) = call(
        second_kernel,
        [(planes, f32, HBM)],
        [rows, pltpu.VMEM(planes, f32), dma((len(GROUPS),))],
        "second",
        (band, SMEM),
        *inside(ghosts, base, partial, deltas, near),
    )
    return updated


def solution(mesh):
    in_specs = (
        P("freq", None, "mesh"),
        P(None, "mesh"),
        P("mesh"),
        P(None, "mesh"),
        P(None, "mesh"),
        P("mesh", None),
        P("mesh"),
    )
    out_specs = P("freq", None, "mesh")
    return jax.shard_map(local, mesh=mesh, in_specs=in_specs, out_specs=out_specs, check_vma=False)
```

```python
import math

import jax
import jax.numpy as jnp
import numpy as np
from jax import lax
from jax.experimental import pallas as pl
from jax.experimental.pallas import tpu as pltpu
from jax.sharding import PartitionSpec as P

NF = 36
ND = 36
K = 8
NP = 512
CAP = 8
N_MESH = 32
GHOSTS = N_MESH * CAP
BAND = 9
UP_REACH = 2
DOWN_REACH = 3
UP_SHIFT = 1
DOWN_SHIFT = 3
COORDS = BAND * ND
ROWS = COORDS + 4
LANES = 384
PAIR = 2 * ND
GROUPS = [(0, PAIR), (PAIR, PAIR), (2 * PAIR, PAIR), (3 * PAIR, PAIR), (4 * PAIR, ROWS - 4 * PAIR)]

time_step = 0.5
group_scale = 0.8
quad_coupling = 0.25
wind_growth = 0.1
RATIOS = np.power(np.float64(1.1), np.arange(NF) - NF // 2)


def rounded(x):
    return x.astype(jnp.bfloat16).astype(jnp.float32)


def bf16_pieces(x):
    high = rounded(x)
    return jnp.concatenate([high, x - high], axis=0).astype(jnp.bfloat16)


def pieces_with_coords(x):
    top = []
    for axis in range(2):
        row = COORDS + 2 * axis
        high = rounded(x[row : row + 1])
        top += [high, x[row : row + 1] - high, x[row + 1 : row + 2]]
    top.append(jnp.zeros((2, x.shape[1]), jnp.float32))
    high = rounded(x)
    return jnp.concatenate([jnp.concatenate(top, axis=0), high, x - high], axis=0).astype(jnp.bfloat16)


def exact_rows(c):
    high = rounded(c)
    mid = rounded(c - high)
    return high + mid, (c - high) - mid


def by_band(band, values):
    picked = jnp.float32(values[3])
    for index in (2, 1, 0):
        picked = jnp.where(band == index, jnp.float32(values[index]), picked)
    return picked


def ratio_of(band, f):
    return by_band(band, [RATIOS[b * BAND + f] for b in range(NF // BAND)])


def scale_of(band, f):
    return by_band(band, [time_step * group_scale / RATIOS[b * BAND + f] for b in range(NF // BAND)])


def one_hot(entry_row, first, count):
    node = lax.broadcasted_iota(jnp.int32, (count, entry_row.shape[1]), 0) + first
    return jnp.where(node == entry_row, 1.0, 0.0).astype(jnp.bfloat16)


def gather(pieces, entry_row, first):
    got = jnp.dot(pieces, one_hot(entry_row, first, pieces.shape[1]), preferred_element_type=jnp.float32)
    top = got.shape[0] - 2 * ROWS
    return got[:top], got[top : top + ROWS] + got[top + ROWS :]


def fill_coords(rows_ref, coords_ref):
    for axis in range(2):
        first, second = exact_rows(coords_ref[axis : axis + 1, :])
        rows_ref[COORDS + 2 * axis : COORDS + 2 * axis + 1, :] = first
        rows_ref[COORDS + 2 * axis + 1 : COORDS + 2 * axis + 2, :] = second


def fill_rows(rows_ref, spectra_ref, coords_ref):
    for f in range(BAND):
        rows_ref[f * ND : (f + 1) * ND, :] = spectra_ref[f]
    fill_coords(rows_ref, coords_ref)


def packing_one_hot(send, count):
    slots = jnp.concatenate([send.astype(jnp.float32)] * N_MESH, axis=0)
    counts = jnp.broadcast_to(count.astype(jnp.float32), slots.shape)
    row = lax.broadcasted_iota(jnp.int32, slots.shape, 0)
    mine = lax.broadcasted_iota(jnp.int32, slots.shape, 1) == N_MESH - 1 - row // CAP
    node = jnp.sum(jnp.where(mine, slots, 0.0), axis=1, keepdims=True)
    used = jnp.sum(jnp.where(mine, counts, 0.0), axis=1, keepdims=True)
    place = lax.broadcasted_iota(jnp.int32, (GHOSTS, 1), 0) % CAP
    node = jnp.where(place.astype(jnp.float32) < used, node, -1.0).astype(jnp.int32)
    return jnp.where(lax.broadcasted_iota(jnp.int32, (GHOSTS, NP), 1) == node, 1.0, 0.0).astype(jnp.bfloat16)


def pack(hot, rows, packed_ref):
    dims = (((1,), (1,)), ((), ()))
    got = lax.dot_general(bf16_pieces(rows), hot, dims, preferred_element_type=jnp.float32)
    packed_ref[:, :ROWS] = (got[:ROWS] + got[ROWS:]).T
    packed_ref[:, ROWS:] = jnp.zeros((GHOSTS, LANES - ROWS), jnp.float32)


def directions():
    place = lax.broadcasted_iota(jnp.int32, (8, 128), 0)
    within = [jnp.full((8, 128), 0.0, jnp.float32)] * 2
    for row in range(8):
        angle = (row + 0.5) * 2.0 * math.pi / ND
        within = [jnp.where(place == row, jnp.float32(g(angle)), old) for g, old in zip((math.cos, math.sin), within)]
    inner_cosine, inner_sine = within
    cosine, sine = [], []
    for tile in range(PAIR // 8):
        angle = 8 * tile * 2.0 * math.pi / ND
        outer_cosine, outer_sine = jnp.float32(math.cos(angle)), jnp.float32(math.sin(angle))
        cosine.append(outer_cosine * inner_cosine - outer_sine * inner_sine)
        sine.append(outer_sine * inner_cosine + outer_cosine * inner_sine)
    return [jnp.concatenate([jnp.concatenate(tiles, axis=0)] * (NP // 128), axis=1) for tiles in (cosine, sine)]


def delta(place, coords, axis):
    row = 3 * axis
    return ((place[row : row + 1] + place[row + 1 : row + 2]) + place[row + 2 : row + 3]) - coords[axis : axis + 1]


def facing(cosine, sine, delta_x, delta_y):
    return jnp.maximum(-(cosine * delta_x + sine * delta_y), 0.0)


def add_slot(target_ref, source_ref, inflow, got, fresh):
    for start, size in GROUPS:
        rows = slice(start, start + size)
        term = inflow[:size] * got[rows]
        target_ref[rows] = term if fresh else source_ref[rows] + term


def rolled(x, shift):
    shift = shift % ND
    return jnp.concatenate([x[ND - shift :], x[: ND - shift]], axis=0)


def pack_kernel(
    band_ref, spectra_hbm, coords_hbm, send_hbm, count_hbm, wind_hbm, area_hbm, near_hbm,
    packed_ref, spectra_ref, coords_ref, send_ref, count_ref, wind_ref, area_ref, near_ref, near_edge_ref, far_edge_ref,
    rows_ref, hot_ref, sems,
):
    odd = lax.rem(band_ref[0], 2)
    inner = pl.ds((1 - odd) * (BAND - DOWN_REACH), DOWN_REACH)
    outer = pl.ds(odd * (BAND - DOWN_REACH), DOWN_REACH)
    pairs = (
        (send_hbm, send_ref),
        (count_hbm, count_ref),
        (spectra_hbm, spectra_ref),
        (coords_hbm, coords_ref),
        (spectra_hbm.at[inner], near_edge_ref),
        (spectra_hbm.at[outer], far_edge_ref),
        (wind_hbm, wind_ref),
        (area_hbm, area_ref),
        (near_hbm, near_ref),
    )
    copies = [pltpu.make_async_copy(source, target, sems.at[i]) for i, (source, target) in enumerate(pairs)]
    for copy in copies:
        copy.start()
    for copy in copies[:2]:
        copy.wait()
    hot_ref[...] = packing_one_hot(send_ref[...], count_ref[...])
    for copy in copies[2:4]:
        copy.wait()
    fill_rows(rows_ref, spectra_ref, coords_ref)
    pack(hot_ref[...], rows_ref[...], packed_ref)
    for copy in copies[4:]:
        copy.wait()
    entry = near_ref[...]
    place = lax.rem(entry, CAP)
    near_ref[...] = jnp.where(entry < NP, entry, NP + (NP + GHOSTS - CAP) - (entry - place) + place)


def source(f, band, spectra_ref, lower_ref, upper_ref, along, base_ref):
    density = spectra_ref[f]
    up = spectra_ref[f + UP_REACH] if f + UP_REACH < BAND else upper_ref[f + UP_REACH - BAND]
    down = spectra_ref[f - DOWN_REACH] if f >= DOWN_REACH else lower_ref[f]
    up_left, up_right = rolled(up, -UP_SHIFT), rolled(up, UP_SHIFT)
    down_left, down_right = rolled(down, DOWN_SHIFT), rolled(down, -DOWN_SHIFT)
    quad = quad_coupling * (
        density * density * (up_left + down_left + up_right + down_right)
        - 2.0 * density * (up_left * down_left + up_right * down_right)
    )
    growth = wind_growth * jnp.maximum(ratio_of(band, f) * along - 1.0, 0.0)
    base_ref[f * ND : (f + 1) * ND] = density + time_step * (quad + growth * density)


def edge_sources(is_lower, edge_ref, band, spectra_ref, along, base_ref):
    @pl.when(is_lower)
    def _():
        for f in range(DOWN_REACH):
            source(f, band, spectra_ref, edge_ref, None, along, base_ref)

    @pl.when(jnp.logical_not(is_lower))
    def _():
        for f in range(BAND - UP_REACH, BAND):
            source(f, band, spectra_ref, None, edge_ref, along, base_ref)


def local_kernel(
    band_ref, spectra_ref, near_edge_ref, coords_ref, wind_ref, area_ref, near_ref, base_ref, partial_ref, rows_ref
):
    band = band_ref[0]
    coords = coords_ref[...]
    fill_rows(rows_ref, spectra_ref, coords_ref)
    pieces = pieces_with_coords(rows_ref[...])
    cosine, sine = directions()
    along = cosine[:ND] * wind_ref[0:1, :] + sine[:ND] * wind_ref[1:2, :]
    base_ref[COORDS:] = jnp.zeros((ROWS - COORDS, NP), jnp.float32)
    for f in range(DOWN_REACH, BAND - UP_REACH):
        source(f, band, spectra_ref, None, None, along, base_ref)
    for k in range(K):
        entry = near_ref[k : k + 1, :]
        place, got = gather(pieces, entry, 0)
        delta_x = jnp.where(entry < NP, delta(place, coords, 0), 0.0)
        delta_y = jnp.where(entry < NP, delta(place, coords, 1), 0.0)
        partial_ref[ROWS + k : ROWS + k + 1] = delta_x
        partial_ref[ROWS + K + k : ROWS + K + k + 1] = delta_y
        add_slot(partial_ref, partial_ref, facing(cosine, sine, delta_x, delta_y), got, k == 0)
    partial_ref[ROWS + 2 * K : ROWS + 2 * K + 1] = area_ref[...]
    edge_sources(lax.rem(band, 2) == 1, near_edge_ref, band, spectra_ref, along, base_ref)


def settle(band, base_ref, area, total_ref, weight, group, target_ref):
    start, size = group
    rows = slice(start, start + size)
    lower, upper = start // ND, min(start // ND + 1, BAND - 1)
    row = lax.broadcasted_iota(jnp.int32, (size, NP), 0)
    scaled = jnp.where(row < ND, scale_of(band, lower), scale_of(band, upper)) * area
    target_ref[rows] = (base_ref[rows] + scaled * total_ref[rows]) / (1.0 + scaled * weight[:size])


def ghost_rows(ghost_ref):
    return ghost_ref[...].T[:ROWS]


def first_gather_kernel(ghost_ref, partial_ref, coords_ref, near_ref, total_ref, weight_ref, delta_ref):
    coords = coords_ref[...]
    pieces = pieces_with_coords(ghost_rows(ghost_ref))
    cosine, sine = directions()
    weight = jnp.zeros((PAIR, NP), jnp.float32)
    for k in range(K):
        entry = near_ref[k : k + 1, :]
        place, got = gather(pieces, entry, NP)
        delta_x = jnp.where(entry < NP, partial_ref[ROWS + k : ROWS + k + 1], delta(place, coords, 0))
        delta_y = jnp.where(entry < NP, partial_ref[ROWS + K + k : ROWS + K + k + 1], delta(place, coords, 1))
        delta_ref[k : k + 1, :] = delta_x
        delta_ref[K + k : K + k + 1, :] = delta_y
        inflow = facing(cosine, sine, delta_x, delta_y)
        weight = weight + inflow
        add_slot(total_ref, partial_ref if k == 0 else total_ref, inflow, got, False)
    weight_ref[...] = weight
    delta_ref[2 * K : 2 * K + 1, :] = partial_ref[ROWS + 2 * K : ROWS + 2 * K + 1]


def first_settle_kernel(
    band_ref, spectra_ref, far_edge_ref, wind_ref, part_ref, total_ref, weight_ref, delta_ref, send_ref, count_ref,
    packed_ref, current_ref, base_ref,
):
    band = band_ref[0]
    cosine, sine = directions()
    along = cosine[:ND] * wind_ref[0:1, :] + sine[:ND] * wind_ref[1:2, :]
    base_ref[...] = part_ref[...]
    edge_sources(lax.rem(band, 2) == 0, far_edge_ref, band, spectra_ref, along, base_ref)
    area, weight = delta_ref[2 * K : 2 * K + 1], weight_ref[...]
    for group in GROUPS:
        settle(band, base_ref, area, total_ref, weight, group, current_ref)
    pack(packing_one_hot(send_ref[...], count_ref[...]), current_ref[...], packed_ref)


def second_local_kernel(current_ref, delta_ref, near_ref, partial_ref):
    pieces = bf16_pieces(current_ref[...])
    cosine, sine = directions()
    for k in range(K):
        _, got = gather(pieces, near_ref[k : k + 1, :], 0)
        inflow = facing(cosine, sine, delta_ref[k : k + 1, :], delta_ref[K + k : K + k + 1, :])
        add_slot(partial_ref, partial_ref, inflow, got, k == 0)


def second_kernel(
    band_ref, ghost_ref, base_ref, partial_ref, delta_ref, near_ref, out_ref, total_ref, planes_ref, sems
):
    band = band_ref[0]
    pieces = bf16_pieces(ghost_rows(ghost_ref))
    cosine, sine = directions()
    weight = jnp.zeros((PAIR, NP), jnp.float32)
    for k in range(K):
        _, got = gather(pieces, near_ref[k : k + 1, :], NP)
        inflow = facing(cosine, sine, delta_ref[k : k + 1, :], delta_ref[K + k : K + k + 1, :])
        weight = weight + inflow
        add_slot(total_ref, partial_ref if k == 0 else total_ref, inflow, got, False)
    area = delta_ref[2 * K : 2 * K + 1, :]
    copies = []
    for index, group in enumerate(GROUPS):
        settle(band, base_ref, area, total_ref, weight, group, total_ref)
        first = 2 * index
        count = min(2, BAND - first)
        for f in range(first, first + count):
            planes_ref[f] = total_ref[f * ND : (f + 1) * ND]
        moved = pl.ds(first, count)
        copies.append(pltpu.make_async_copy(planes_ref.at[moved], out_ref.at[moved], sems.at[index]))
        copies[-1].start()
    for copy in copies:
        copy.wait()


VMEM, SMEM, HBM = pltpu.VMEM, pltpu.SMEM, pltpu.HBM


def call(kernel, outs, scratch, name, *operands):
    return pl.pallas_call(
        kernel,
        out_shape=[jax.ShapeDtypeStruct(shape, dtype) for shape, dtype, _ in outs],
        in_specs=[pl.BlockSpec(memory_space=memory) for _, memory in operands],
        out_specs=[pl.BlockSpec(memory_space=memory) for _, _, memory in outs],
        scratch_shapes=scratch,
        compiler_params=pltpu.CompilerParams(vmem_limit_bytes=24 << 20),
        name=name,
    )(*[pltpu.with_memory_space_constraint(array, HBM) if memory is HBM else array for array, memory in operands])


def local(spectra, coords, inv_area, wind_vector, neighbours, send_nodes, send_count):
    bands = lax.axis_size("freq")
    band = lax.axis_index("freq").astype(jnp.int32).reshape(1)
    f32, planes = jnp.float32, (BAND, ND, NP)
    rows, dma = pltpu.VMEM((ROWS, NP), f32), pltpu.SemaphoreType.DMA
    send, count, area = send_nodes.T, send_count.reshape(1, -1), inv_area.reshape(1, -1)

    def exchange(packed):
        packed = packed.reshape(N_MESH, CAP, LANES)
        return lax.all_to_all(
            packed, "mesh", split_axis=0, concat_axis=0, tiled=True, axis_index_groups=[list(range(N_MESH))[::-1]]
        ).reshape(GHOSTS, LANES)

    def inside(*arrays):
        return [(array, VMEM) for array in arrays]

    inputs = (spectra, coords, send, count, wind_vector, area, neighbours)
    packed, spectra, coords, send, count, wind, area, near, near_edge, far_edge = call(
        pack_kernel,
        [((GHOSTS, LANES), f32, VMEM)]
        + [(array.shape, array.dtype, VMEM) for array in inputs]
        + [((DOWN_REACH, ND, NP), f32, VMEM)] * 2,
        [rows, pltpu.VMEM((GHOSTS, NP), jnp.bfloat16), dma((len(inputs) + 2,))],
        "pack",
        (band, SMEM),
        *[(array, HBM) for array in inputs],
    )
    pairs = [[pair for i in range(start, bands - 1, 2) for pair in ((i, i + 1), (i + 1, i))] for start in (0, 1)]
    near_edge = lax.ppermute(near_edge, "freq", pairs[0])
    far_edge = lax.ppermute(far_edge, "freq", pairs[1])
    ghosts = exchange(packed)
    base, partial = call(
        local_kernel,
        [((ROWS, NP), f32, VMEM), ((ROWS + 3 * K, NP), f32, VMEM)],
        [rows],
        "local_first",
        (band, SMEM),
        *inside(spectra, near_edge, coords, wind, area, near),
    )
    total, weight, deltas = call(
        first_gather_kernel,
        [((ROWS, NP), f32, VMEM), ((PAIR, NP), f32, VMEM), ((3 * K, NP), f32, VMEM)],
        [],
        "first_gather",
        *inside(ghosts, partial, coords, near),
    )
    packed, current, base = call(
        first_settle_kernel,
        [((GHOSTS, LANES), f32, VMEM), ((ROWS, NP), f32, VMEM), ((ROWS, NP), f32, VMEM)],
        [],
        "first_settle",
        (band, SMEM),
        *inside(spectra, far_edge, wind, base, total, weight, deltas, send, count),
    )
    ghosts = exchange(packed)
    (partial,) = call(
        second_local_kernel, [((ROWS, NP), f32, VMEM)], [], "local_second", *inside(current, deltas, near)
    )
    (updated,) = call(
        second_kernel,
        [(planes, f32, HBM)],
        [rows, pltpu.VMEM(planes, f32), dma((len(GROUPS),))],
        "second",
        (band, SMEM),
        *inside(ghosts, base, partial, deltas, near),
    )
    return updated


def solution(mesh):
    in_specs = (
        P("freq", None, "mesh"),
        P(None, "mesh"),
        P("mesh"),
        P(None, "mesh"),
        P(None, "mesh"),
        P("mesh", None),
        P("mesh"),
    )
    out_specs = P("freq", None, "mesh")
    return jax.shard_map(local, mesh=mesh, in_specs=in_specs, out_specs=out_specs, check_vma=False)
```

```python
import math

import jax
import jax.numpy as jnp
import numpy as np
from jax import lax
from jax.experimental import pallas as pl
from jax.experimental.pallas import tpu as pltpu
from jax.sharding import PartitionSpec as P

NF = 36
ND = 36
K = 8
NP = 512
CAP = 8
N_MESH = 32
GHOSTS = N_MESH * CAP
BAND = 9
UP_REACH = 2
DOWN_REACH = 3
UP_SHIFT = 1
DOWN_SHIFT = 3
COORDS = BAND * ND
ROWS = COORDS + 4
LANES = 384
PAIR = 2 * ND
GROUPS = [(0, PAIR), (PAIR, PAIR), (2 * PAIR, PAIR), (3 * PAIR, PAIR), (4 * PAIR, ROWS - 4 * PAIR)]

time_step = 0.5
group_scale = 0.8
quad_coupling = 0.25
wind_growth = 0.1
RATIOS = np.power(np.float64(1.1), np.arange(NF) - NF // 2)


def rounded(x):
    return x.astype(jnp.bfloat16).astype(jnp.float32)


def bf16_pieces(x):
    high = rounded(x)
    return jnp.concatenate([high, x - high], axis=0).astype(jnp.bfloat16)


def pieces_with_coords(x):
    top = []
    for axis in range(2):
        row = COORDS + 2 * axis
        high = rounded(x[row : row + 1])
        top += [high, x[row : row + 1] - high, x[row + 1 : row + 2]]
    top.append(jnp.zeros((2, x.shape[1]), jnp.float32))
    high = rounded(x)
    return jnp.concatenate([jnp.concatenate(top, axis=0), high, x - high], axis=0).astype(jnp.bfloat16)


def exact_rows(c):
    high = rounded(c)
    mid = rounded(c - high)
    return high + mid, (c - high) - mid


def by_band(band, values):
    picked = jnp.float32(values[3])
    for index in (2, 1, 0):
        picked = jnp.where(band == index, jnp.float32(values[index]), picked)
    return picked


def ratio_of(band, f):
    return by_band(band, [RATIOS[b * BAND + f] for b in range(NF // BAND)])


def scale_of(band, f):
    return by_band(band, [time_step * group_scale / RATIOS[b * BAND + f] for b in range(NF // BAND)])


def one_hot(entry_row, first, count):
    node = lax.broadcasted_iota(jnp.int32, (count, entry_row.shape[1]), 0) + first
    return jnp.where(node == entry_row, 1.0, 0.0).astype(jnp.bfloat16)


def gather(pieces, entry_row, first):
    got = jnp.dot(pieces, one_hot(entry_row, first, pieces.shape[1]), preferred_element_type=jnp.float32)
    top = got.shape[0] - 2 * ROWS
    return got[:top], got[top : top + ROWS] + got[top + ROWS :]


def fill_coords(rows_ref, coords_ref):
    for axis in range(2):
        first, second = exact_rows(coords_ref[axis : axis + 1, :])
        rows_ref[COORDS + 2 * axis : COORDS + 2 * axis + 1, :] = first
        rows_ref[COORDS + 2 * axis + 1 : COORDS + 2 * axis + 2, :] = second


def fill_rows(rows_ref, spectra_ref, coords_ref):
    for f in range(BAND):
        rows_ref[f * ND : (f + 1) * ND, :] = spectra_ref[f]
    fill_coords(rows_ref, coords_ref)


def packing_one_hot(send, count):
    slots = jnp.concatenate([send.astype(jnp.float32)] * N_MESH, axis=0)
    counts = jnp.broadcast_to(count.astype(jnp.float32), slots.shape)
    row = lax.broadcasted_iota(jnp.int32, slots.shape, 0)
    mine = lax.broadcasted_iota(jnp.int32, slots.shape, 1) == jnp.bitwise_xor(row // CAP, 22)
    node = jnp.sum(jnp.where(mine, slots, 0.0), axis=1, keepdims=True)
    used = jnp.sum(jnp.where(mine, counts, 0.0), axis=1, keepdims=True)
    place = lax.broadcasted_iota(jnp.int32, (GHOSTS, 1), 0) % CAP
    node = jnp.where(place.astype(jnp.float32) < used, node, -1.0).astype(jnp.int32)
    return jnp.where(lax.broadcasted_iota(jnp.int32, (GHOSTS, NP), 1) == node, 1.0, 0.0).astype(jnp.bfloat16)


def pack(hot, rows, packed_ref):
    dims = (((1,), (1,)), ((), ()))
    got = lax.dot_general(bf16_pieces(rows), hot, dims, preferred_element_type=jnp.float32)
    packed_ref[:, :ROWS] = (got[:ROWS] + got[ROWS:]).T
    packed_ref[:, ROWS:] = jnp.zeros((GHOSTS, LANES - ROWS), jnp.float32)


def directions():
    place = lax.broadcasted_iota(jnp.int32, (8, 128), 0)
    within = [jnp.full((8, 128), 0.0, jnp.float32)] * 2
    for row in range(8):
        angle = (row + 0.5) * 2.0 * math.pi / ND
        within = [jnp.where(place == row, jnp.float32(g(angle)), old) for g, old in zip((math.cos, math.sin), within)]
    inner_cosine, inner_sine = within
    cosine, sine = [], []
    for tile in range(PAIR // 8):
        angle = 8 * tile * 2.0 * math.pi / ND
        outer_cosine, outer_sine = jnp.float32(math.cos(angle)), jnp.float32(math.sin(angle))
        cosine.append(outer_cosine * inner_cosine - outer_sine * inner_sine)
        sine.append(outer_sine * inner_cosine + outer_cosine * inner_sine)
    return [jnp.concatenate([jnp.concatenate(tiles, axis=0)] * (NP // 128), axis=1) for tiles in (cosine, sine)]


def delta(place, coords, axis):
    row = 3 * axis
    return ((place[row : row + 1] + place[row + 1 : row + 2]) + place[row + 2 : row + 3]) - coords[axis : axis + 1]


def facing(cosine, sine, delta_x, delta_y):
    return jnp.maximum(-(cosine * delta_x + sine * delta_y), 0.0)


def add_slot(target_ref, source_ref, inflow, got, fresh):
    for start, size in GROUPS:
        rows = slice(start, start + size)
        term = inflow[:size] * got[rows]
        target_ref[rows] = term if fresh else source_ref[rows] + term


def rolled(x, shift):
    shift = shift % ND
    return jnp.concatenate([x[ND - shift :], x[: ND - shift]], axis=0)


def pack_kernel(
    band_ref, spectra_hbm, coords_hbm, send_hbm, count_hbm, wind_hbm, area_hbm, near_hbm,
    packed_ref, spectra_ref, coords_ref, send_ref, count_ref, wind_ref, area_ref, near_ref, near_edge_ref, far_edge_ref,
    rows_ref, hot_ref, sems,
):
    odd = lax.rem(band_ref[0], 2)
    inner = pl.ds((1 - odd) * (BAND - DOWN_REACH), DOWN_REACH)
    outer = pl.ds(odd * (BAND - DOWN_REACH), DOWN_REACH)
    pairs = (
        (send_hbm, send_ref),
        (count_hbm, count_ref),
        (spectra_hbm, spectra_ref),
        (coords_hbm, coords_ref),
        (spectra_hbm.at[inner], near_edge_ref),
        (spectra_hbm.at[outer], far_edge_ref),
        (wind_hbm, wind_ref),
        (area_hbm, area_ref),
        (near_hbm, near_ref),
    )
    copies = [pltpu.make_async_copy(source, target, sems.at[i]) for i, (source, target) in enumerate(pairs)]
    for copy in copies:
        copy.start()
    for copy in copies[:2]:
        copy.wait()
    hot_ref[...] = packing_one_hot(send_ref[...], count_ref[...])
    for copy in copies[2:4]:
        copy.wait()
    fill_rows(rows_ref, spectra_ref, coords_ref)
    pack(hot_ref[...], rows_ref[...], packed_ref)
    for copy in copies[4:]:
        copy.wait()
    entry = near_ref[...]
    near_ref[...] = jnp.where(entry < NP, entry, NP + jnp.bitwise_xor(entry - NP, 22 * CAP))


def source(f, band, spectra_ref, lower_ref, upper_ref, along, base_ref):
    density = spectra_ref[f]
    up = spectra_ref[f + UP_REACH] if f + UP_REACH < BAND else upper_ref[f + UP_REACH - BAND]
    down = spectra_ref[f - DOWN_REACH] if f >= DOWN_REACH else lower_ref[f]
    up_left, up_right = rolled(up, -UP_SHIFT), rolled(up, UP_SHIFT)
    down_left, down_right = rolled(down, DOWN_SHIFT), rolled(down, -DOWN_SHIFT)
    quad = quad_coupling * (
        density * density * (up_left + down_left + up_right + down_right)
        - 2.0 * density * (up_left * down_left + up_right * down_right)
    )
    growth = wind_growth * jnp.maximum(ratio_of(band, f) * along - 1.0, 0.0)
    base_ref[f * ND : (f + 1) * ND] = density + time_step * (quad + growth * density)


def edge_sources(is_lower, edge_ref, band, spectra_ref, along, base_ref):
    @pl.when(is_lower)
    def _():
        for f in range(DOWN_REACH):
            source(f, band, spectra_ref, edge_ref, None, along, base_ref)

    @pl.when(jnp.logical_not(is_lower))
    def _():
        for f in range(BAND - UP_REACH, BAND):
            source(f, band, spectra_ref, None, edge_ref, along, base_ref)


def local_kernel(
    band_ref, spectra_ref, near_edge_ref, coords_ref, wind_ref, area_ref, near_ref, base_ref, partial_ref, rows_ref
):
    band = band_ref[0]
    coords = coords_ref[...]
    fill_rows(rows_ref, spectra_ref, coords_ref)
    pieces = pieces_with_coords(rows_ref[...])
    cosine, sine = directions()
    along = cosine[:ND] * wind_ref[0:1, :] + sine[:ND] * wind_ref[1:2, :]
    base_ref[COORDS:] = jnp.zeros((ROWS - COORDS, NP), jnp.float32)
    for k in range(K):
        entry = near_ref[k : k + 1, :]
        place, got = gather(pieces, entry, 0)
        delta_x = jnp.where(entry < NP, delta(place, coords, 0), 0.0)
        delta_y = jnp.where(entry < NP, delta(place, coords, 1), 0.0)
        partial_ref[ROWS + k : ROWS + k + 1] = delta_x
        partial_ref[ROWS + K + k : ROWS + K + k + 1] = delta_y
        add_slot(partial_ref, partial_ref, facing(cosine, sine, delta_x, delta_y), got, k == 0)
    partial_ref[ROWS + 2 * K : ROWS + 2 * K + 1] = area_ref[...]
    edge_sources(lax.rem(band, 2) == 1, near_edge_ref, band, spectra_ref, along, base_ref)


def settle(band, base_ref, area, total_ref, weight, group, target_ref):
    start, size = group
    rows = slice(start, start + size)
    lower, upper = start // ND, min(start // ND + 1, BAND - 1)
    row = lax.broadcasted_iota(jnp.int32, (size, NP), 0)
    scaled = jnp.where(row < ND, scale_of(band, lower), scale_of(band, upper)) * area
    target_ref[rows] = (base_ref[rows] + scaled * total_ref[rows]) / (1.0 + scaled * weight[:size])


def ghost_rows(ghost_ref):
    return ghost_ref[...].T[:ROWS]


def first_gather_kernel(ghost_ref, partial_ref, coords_ref, near_ref, total_ref, weight_ref, delta_ref):
    coords = coords_ref[...]
    pieces = pieces_with_coords(ghost_rows(ghost_ref))
    cosine, sine = directions()
    weight = jnp.zeros((PAIR, NP), jnp.float32)
    for k in range(K):
        entry = near_ref[k : k + 1, :]
        place, got = gather(pieces, entry, NP)
        delta_x = jnp.where(entry < NP, partial_ref[ROWS + k : ROWS + k + 1], delta(place, coords, 0))
        delta_y = jnp.where(entry < NP, partial_ref[ROWS + K + k : ROWS + K + k + 1], delta(place, coords, 1))
        delta_ref[k : k + 1, :] = delta_x
        delta_ref[K + k : K + k + 1, :] = delta_y
        inflow = facing(cosine, sine, delta_x, delta_y)
        weight = weight + inflow
        add_slot(total_ref, partial_ref if k == 0 else total_ref, inflow, got, False)
    weight_ref[...] = weight
    delta_ref[2 * K : 2 * K + 1, :] = partial_ref[ROWS + 2 * K : ROWS + 2 * K + 1]


def first_settle_kernel(
    band_ref, spectra_ref, far_edge_ref, wind_ref, part_ref, total_ref, weight_ref, delta_ref, send_ref, count_ref,
    packed_ref, current_ref, base_ref,
):
    band = band_ref[0]
    cosine, sine = directions()
    along = cosine[:ND] * wind_ref[0:1, :] + sine[:ND] * wind_ref[1:2, :]
    base_ref[...] = part_ref[...]
    for f in range(DOWN_REACH, BAND - UP_REACH):
        source(f, band, spectra_ref, None, None, along, base_ref)
    edge_sources(lax.rem(band, 2) == 0, far_edge_ref, band, spectra_ref, along, base_ref)
    area, weight = delta_ref[2 * K : 2 * K + 1], weight_ref[...]
    for group in GROUPS:
        settle(band, base_ref, area, total_ref, weight, group, current_ref)
    pack(packing_one_hot(send_ref[...], count_ref[...]), current_ref[...], packed_ref)


def second_local_kernel(current_ref, delta_ref, near_ref, partial_ref):
    pieces = bf16_pieces(current_ref[...])
    cosine, sine = directions()
    for k in range(K):
        _, got = gather(pieces, near_ref[k : k + 1, :], 0)
        inflow = facing(cosine, sine, delta_ref[k : k + 1, :], delta_ref[K + k : K + k + 1, :])
        add_slot(partial_ref, partial_ref, inflow, got, k == 0)


def second_kernel(
    band_ref, ghost_ref, base_ref, partial_ref, delta_ref, near_ref, out_ref, total_ref, planes_ref, sems
):
    band = band_ref[0]
    pieces = bf16_pieces(ghost_rows(ghost_ref))
    cosine, sine = directions()
    weight = jnp.zeros((PAIR, NP), jnp.float32)
    for k in range(K):
        _, got = gather(pieces, near_ref[k : k + 1, :], NP)
        inflow = facing(cosine, sine, delta_ref[k : k + 1, :], delta_ref[K + k : K + k + 1, :])
        weight = weight + inflow
        add_slot(total_ref, partial_ref if k == 0 else total_ref, inflow, got, False)
    area = delta_ref[2 * K : 2 * K + 1, :]
    copies = []
    for index, group in enumerate(GROUPS):
        settle(band, base_ref, area, total_ref, weight, group, total_ref)
        first = 2 * index
        count = min(2, BAND - first)
        for f in range(first, first + count):
            planes_ref[f] = total_ref[f * ND : (f + 1) * ND]
        moved = pl.ds(first, count)
        copies.append(pltpu.make_async_copy(planes_ref.at[moved], out_ref.at[moved], sems.at[index]))
        copies[-1].start()
    for copy in copies:
        copy.wait()


VMEM, SMEM, HBM = pltpu.VMEM, pltpu.SMEM, pltpu.HBM


def call(kernel, outs, scratch, name, *operands):
    return pl.pallas_call(
        kernel,
        out_shape=[jax.ShapeDtypeStruct(shape, dtype) for shape, dtype, _ in outs],
        in_specs=[pl.BlockSpec(memory_space=memory) for _, memory in operands],
        out_specs=[pl.BlockSpec(memory_space=memory) for _, _, memory in outs],
        scratch_shapes=scratch,
        compiler_params=pltpu.CompilerParams(vmem_limit_bytes=24 << 20),
        name=name,
    )(*[pltpu.with_memory_space_constraint(array, HBM) if memory is HBM else array for array, memory in operands])


def local(spectra, coords, inv_area, wind_vector, neighbours, send_nodes, send_count):
    bands = lax.axis_size("freq")
    band = lax.axis_index("freq").astype(jnp.int32).reshape(1)
    f32, planes = jnp.float32, (BAND, ND, NP)
    rows, dma = pltpu.VMEM((ROWS, NP), f32), pltpu.SemaphoreType.DMA
    send, count, area = send_nodes.T, send_count.reshape(1, -1), inv_area.reshape(1, -1)

    def exchange(packed):
        packed = packed.reshape(N_MESH, CAP, LANES)
        return lax.all_to_all(
            packed, "mesh", split_axis=0, concat_axis=0, tiled=True, axis_index_groups=[[i ^ 22 for i in range(N_MESH)]]
        ).reshape(GHOSTS, LANES)

    def inside(*arrays):
        return [(array, VMEM) for array in arrays]

    inputs = (spectra, coords, send, count, wind_vector, area, neighbours)
    packed, spectra, coords, send, count, wind, area, near, near_edge, far_edge = call(
        pack_kernel,
        [((GHOSTS, LANES), f32, VMEM)]
        + [(array.shape, array.dtype, VMEM) for array in inputs]
        + [((DOWN_REACH, ND, NP), f32, VMEM)] * 2,
        [rows, pltpu.VMEM((GHOSTS, NP), jnp.bfloat16), dma((len(inputs) + 2,))],
        "pack",
        (band, SMEM),
        *[(array, HBM) for array in inputs],
    )
    pairs = [[pair for i in range(start, bands - 1, 2) for pair in ((i, i + 1), (i + 1, i))] for start in (0, 1)]
    near_edge = lax.ppermute(near_edge, "freq", pairs[0])
    far_edge = lax.ppermute(far_edge, "freq", pairs[1])
    ghosts = exchange(packed)
    base, partial = call(
        local_kernel,
        [((ROWS, NP), f32, VMEM), ((ROWS + 3 * K, NP), f32, VMEM)],
        [rows],
        "local_first",
        (band, SMEM),
        *inside(spectra, near_edge, coords, wind, area, near),
    )
    total, weight, deltas = call(
        first_gather_kernel,
        [((ROWS, NP), f32, VMEM), ((PAIR, NP), f32, VMEM), ((3 * K, NP), f32, VMEM)],
        [],
        "first_gather",
        *inside(ghosts, partial, coords, near),
    )
    packed, current, base = call(
        first_settle_kernel,
        [((GHOSTS, LANES), f32, VMEM), ((ROWS, NP), f32, VMEM), ((ROWS, NP), f32, VMEM)],
        [],
        "first_settle",
        (band, SMEM),
        *inside(spectra, far_edge, wind, base, total, weight, deltas, send, count),
    )
    ghosts = exchange(packed)
    (partial,) = call(
        second_local_kernel, [((ROWS, NP), f32, VMEM)], [], "local_second", *inside(current, deltas, near)
    )
    (updated,) = call(
        second_kernel,
        [(planes, f32, HBM)],
        [rows, pltpu.VMEM(planes, f32), dma((len(GROUPS),))],
        "second",
        (band, SMEM),
        *inside(ghosts, base, partial, deltas, near),
    )
    return updated


def solution(mesh):
    in_specs = (
        P("freq", None, "mesh"),
        P(None, "mesh"),
        P("mesh"),
        P(None, "mesh"),
        P(None, "mesh"),
        P("mesh", None),
        P("mesh"),
    )
    out_specs = P("freq", None, "mesh")
    return jax.shard_map(local, mesh=mesh, in_specs=in_specs, out_specs=out_specs, check_vma=False)
```
